512 devices in a mesh: rows: 512 (over y, z, x, core).
Axes of the slice: x: 4, y: 4, z: 16, core: 2. Of those that a mesh axis runs over, the one named last changes fastest.
Arguments:
- right_side: float32 [64, 131072], P(None, 'rows'), may hold values from -6 to 6
- blocks: float32 [7, 64, 131072], P(None, None, 'rows'), may hold values from -0.18898223 to 0.18898223
- cols: int32 [7, 2048], P(None, 'rows'), may hold values from 0 to 2047, as said below
Outputs:
- update: float32 [64, 131072], P(None, 'rows')
- new_residual: float32 [64, 131072], P(None, 'rows')
The draws below stay inside these ranges and needn't reach their ends.
Inputs may be any that keep to these rules, and one draw needn't show every extreme that they name: For block row i, cols[0, i] = i, cols[1, i] and cols[2, i] are i + 1 and i - 1, cols[3, i] and cols[4, i] are i + 1 and i - 1, and cols[5, i], cols[6, i] lie within 1 of i, all modulo 2048.
All inputs are finite; a program needn't handle non-finite values.
Results may differ from the reference program's by a relative error of at most 0.00026.
Values sent between devices are 32-bit elements; how exact they have to be, the bound alone decides.
No kernel may reach another device: no remote copies, remote signals or barrier semaphores. Data moves between devices by JAX's collectives and lax.ppermute only.
A program may use at most 64 MiB of HBM per device.

```python
import jax
import jax.numpy as jnp
from jax import lax

BS = 64
RHS = 64
SLOTS = 7
S = 4
REACH = 1
NBLK = 2048
DOFS = 131072


def draw_cols(key, part):
    rows_all = jnp.arange(NBLK, dtype=jnp.int32)
    near = jax.random.randint(jax.random.fold_in(key, 11), (2, NBLK), -REACH, REACH + 1).astype(jnp.int32)
    fixed_offsets = jnp.array([0, 1, -1, 0, 0], jnp.int32)
    fixed_offsets = fixed_offsets + jnp.array([0, 0, 0, 1, -1], jnp.int32) * REACH
    offsets = jnp.concatenate([jnp.broadcast_to(fixed_offsets[:, None], (5, NBLK)), near], axis=0)
    return jnp.mod(rows_all[None, :] + offsets, NBLK).astype(jnp.int32)


def levels(rng, shape, shards, low, top_value):
    def one(dim, parts):
        draws = jax.random.uniform(jax.random.fold_in(jax.random.fold_in(rng, 6), dim), (parts,), jnp.float32, low / len(shards), top_value / len(shards))
        return jnp.repeat(jnp.exp(draws), shape[dim] // parts).reshape((-1,) + (1,) * (len(shape) - dim - 1))

    gain = one(*shards[0])
    for cut in shards[1:]:
        gain = gain * one(*cut)
    return gain


def centred(own_key, shape, deviation, limit, cuts=(), kind=jnp.bfloat16):
    drawn = jax.random.normal(own_key, shape, jnp.float32) * deviation
    if len(cuts) > 0:
        drawn = levels(own_key, shape, cuts, -0.22, 0.18) * drawn
    return jnp.clip(drawn, min=-limit, max=limit).astype(kind)


def setup_inputs(seed: int = 0) -> dict:
    key_list = jax.random.split(jax.random.key(seed), 4)
    return {
        "right_side": centred(key_list[0], (RHS, DOFS), 1.0, 6.0, ((1, 512),), jnp.float32),
        "blocks": centred(key_list[1], (SLOTS, BS, DOFS), (0.8 / (SLOTS * BS) ** 0.5), 0.18898223, ((2, 512),), jnp.float32),
        "cols": draw_cols(jax.random.fold_in(key_list[3], 71), 0),
    }


SCALE = 1.25

def multiply(vector, blocks, cols):
    sources = vector.shape[0]
    width = blocks.shape[1]
    shaped = vector.reshape(sources, -1, width)
    count = cols.shape[1]
    total = jnp.zeros((sources, count, width), jnp.float32)
    for slot in range(cols.shape[0]):
        picked = jnp.take(shaped, cols[slot], axis=1)
        matrix = blocks[slot].reshape(width, count, width)
        total = total + jnp.einsum('cir,aic->air', matrix, picked, precision=lax.Precision.HIGHEST)
    return total.reshape(sources, count * width)

def finish(right_side, stack, gram):
    sources = right_side.shape[0]
    order = stack.shape[0]
    mixing = jnp.eye(order, order - sources, dtype=jnp.float32) + jnp.eye(order, order - sources, k=-sources, dtype=jnp.float32) / SCALE
    high = lax.Precision.HIGHEST
    folded = jnp.dot(mixing.T.astype(jnp.float32), gram.astype(jnp.float32), precision=high, preferred_element_type=jnp.float32)
    normal = jnp.dot(folded.astype(jnp.float32), mixing.astype(jnp.float32), precision=high, preferred_element_type=jnp.float32)
    target = folded[:, :sources]
    factor = jnp.linalg.cholesky(normal)
    coeff = jax.scipy.linalg.cho_solve((factor, True), target)
    dims = (((0,), (0,)), ((), ()))
    update = lax.dot_general(coeff.astype(jnp.float32), stack[:order - sources].astype(jnp.float32), dims, precision=high, preferred_element_type=jnp.float32)
    images = stack[:order - sources] + stack[sources:] / SCALE
    new_residual = right_side - lax.dot_general(coeff.astype(jnp.float32), images.astype(jnp.float32), dims, precision=high, preferred_element_type=jnp.float32)
    return (update, new_residual)

def reference(right_side, blocks, cols):
    powers = [right_side]
    current = right_side
    for step in range(S):
        current = SCALE * multiply(current, blocks, cols)
        powers.append(current)
    stack = jnp.concatenate(powers, axis=0)
    gram = lax.dot_general(stack.astype(jnp.float32), stack.astype(jnp.float32), (((1,), (1,)), ((), ())), precision=lax.Precision.HIGHEST, preferred_element_type=jnp.float32)
    update, new_residual = finish(right_side, stack, gram)
    return (update, new_residual)
```

```python
import functools

import jax
import jax.numpy as jnp
from jax import lax
from jax.experimental import pallas as pl
from jax.experimental.pallas import tpu as pltpu
from jax.sharding import Mesh, PartitionSpec as P

SCALE = 1.25
S = 4
BS = 64
HIGH = lax.Precision.HIGHEST

VMEM = pl.BlockSpec(memory_space=pltpu.VMEM)
SMEM = pl.BlockSpec(memory_space=pltpu.SMEM)


def dot(a, b, dims):
    return lax.dot_general(a, b, (dims, ((), ())), precision=HIGH, preferred_element_type=jnp.float32)


def pack_kernel(total_blocks, cols_ref, right_ref, blocks_ref, out_ref):
    width = right_ref.shape[1]
    lane = lax.broadcasted_iota(jnp.int32, (1, width), 1) // BS
    minus = blocks_ref[2] + blocks_ref[4]
    zero = blocks_ref[0]
    plus = blocks_ref[1] + blocks_ref[3]
    for slot in (5, 6):
        offset = jnp.zeros((1, width), jnp.int32)
        for row in range(width // BS):
            delta = cols_ref[slot, row] - cols_ref[0, row]
            delta = jnp.where(delta > 1, delta - total_blocks, delta)
            delta = jnp.where(delta < -1, delta + total_blocks, delta)
            offset = jnp.where(lane == row, delta, offset)
        matrix = blocks_ref[slot]
        minus = minus + jnp.where(offset == -1, matrix, 0.0)
        zero = zero + jnp.where(offset == 0, matrix, 0.0)
        plus = plus + jnp.where(offset == 1, matrix, 0.0)
    out_ref[0:64, :] = minus
    out_ref[64:128, :] = zero
    out_ref[128:192, :] = plus
    out_ref[192:256, :] = right_ref[...]


def basis_kernel(cols_ref, own_ref, pair_ref, other_ref, sums_ref, stack_ref, ext_ref, band_ref):
    even = lax.rem(cols_ref[0, 0] // 4, 2) == 0

    @pl.when(even)
    def _():
        ext_ref[:, 0:256] = other_ref[...]
        ext_ref[:, 512:768] = pair_ref[...]

    @pl.when(jnp.logical_not(even))
    def _():
        ext_ref[:, 0:256] = pair_ref[...]
        ext_ref[:, 512:768] = other_ref[...]

    ext_ref[:, 256:512] = own_ref[...]
    left = lax.broadcasted_iota(jnp.int32, (BS, 128), 1) < BS
    for p in range(6):
        at = slice(128 * p, 128 * (p + 1))
        minus, zero, plus = ext_ref[0:64, at], ext_ref[64:128, at], ext_ref[128:192, at]
        band_ref[p, 0:64, :] = jnp.where(left, minus, 0.0)
        band_ref[p, 64:128, :] = jnp.where(left, zero, minus)
        band_ref[p, 128:192, :] = jnp.where(left, plus, zero)
        band_ref[p, 192:256, :] = jnp.where(left, 0.0, plus)
    current = ext_ref[192:256, :]
    first = 0
    own = [current[:, 256:512]]
    images = []
    for step, (low, high) in enumerate(((0, 6), (1, 5), (1, 5), (2, 4))):
        rolled = pltpu.roll(current, 64, 1)
        parts = []
        for p in range(low, high):
            at = 128 * (p - first)
            if at + 256 <= rolled.shape[1]:
                window = rolled[:, at : at + 256]
            else:
                window = jnp.concatenate([rolled[:, at:], rolled[:, :128]], axis=1)
            parts.append(dot(window, band_ref[p], ((1,), (0,))))
        product = jnp.concatenate(parts, axis=1)
        inner = product[:, 256 - 128 * low : 512 - 128 * low]
        images.append(own[step] + inner)
        current = SCALE * product
        first = low
        own.append(SCALE * inner)
    w = jnp.concatenate(images, axis=0)
    stack_ref[:, 0:256] = jnp.concatenate(own[:S], axis=0)
    stack_ref[:, 256:512] = w
    gram = dot(w, jnp.concatenate([own[0], w], axis=0), ((1,), (1,)))
    sums_ref[0:64, :] = gram[0:64, 0:128]
    sums_ref[64:128, :] = gram[64:128, 0:128]
    sums_ref[128:192, :] = gram[128:192, 0:128]
    sums_ref[192:256, :] = gram[128:192, 128:256]
    sums_ref[256:320, :] = gram[192:256, 0:128]
    sums_ref[320:384, :] = gram[192:256, 128:256]
    sums_ref[384:448, :] = jnp.concatenate([gram[64:128, 128:192], gram[192:256, 256:320]], axis=1)
    sums_ref[448:512, :] = jnp.zeros((64, 128), jnp.float32)


def total_kernel(copies, in_ref, out_ref):
    total = in_ref[0]
    for k in range(1, in_ref.shape[0]):
        total = total + in_ref[k]
    for k in range(copies):
        out_ref[k] = total


def eliminate(block):
    rows = lax.broadcasted_iota(jnp.int32, (BS, 1), 0)
    for k in range(BS):
        pivot_row = block[k : k + 1, :] / block[k : k + 1, k : k + 1]
        factor = jnp.where(rows == k, 0.0, block[:, k : k + 1])
        block = jnp.where(rows == k, pivot_row, block - factor * pivot_row)
    return block


def solve_kernel(sums_ref, stack_ref, right_ref, update_ref, residual_ref):
    u = [sums_ref[64 * k : 64 * (k + 1), :] for k in range(7)]
    t = [u[0][:, 0:64], u[1][:, 0:64], u[2][:, 0:64], u[4][:, 0:64]]
    n = {}
    n[0, 0] = u[0][:, 64:128]
    n[1, 0] = u[1][:, 64:128]
    n[1, 1] = u[6][:, 0:64]
    n[2, 0] = u[2][:, 64:128]
    n[2, 1] = u[3][:, 0:64]
    n[2, 2] = u[3][:, 64:128]
    n[3, 0] = u[4][:, 64:128]
    n[3, 1] = u[5][:, 0:64]
    n[3, 2] = u[5][:, 64:128]
    n[3, 3] = u[6][:, 64:128]
    done = []
    for k in range(S):
        below = [n[i, k] for i in range(k + 1, S)]
        wide = [n[k, k]] + [b.T for b in below] + [t[k]]
        wide = eliminate(jnp.concatenate(wide, axis=1))
        done.append(wide)
        for i in range(k + 1, S):
            change = dot(n[i, k], wide, ((1,), (0,)))
            for j in range(k + 1, i + 1):
                n[i, j] = n[i, j] - change[:, 64 * (j - k) : 64 * (j - k + 1)]
            t[i] = t[i] - change[:, 64 * (S - k) : 64 * (S - k + 1)]
    x = [None] * S
    for k in range(S - 1, -1, -1):
        x[k] = done[k][:, 64 * (S - k) : 64 * (S - k + 1)]
        for j in range(k + 1, S):
            x[k] = x[k] - dot(done[k][:, 64 * (j - k) : 64 * (j - k + 1)], x[j], ((1,), (0,)))
    coeff = jnp.concatenate(x, axis=0)
    both = dot(coeff, stack_ref[...], ((0,), (0,)))
    update_ref[...] = both[:, 0:256]
    residual_ref[...] = right_ref[...] - both[:, 256:512]


def call(kernel, outs, in_specs, scratch=(), name=None):
    shapes = [jax.ShapeDtypeStruct(s, jnp.float32) for s in outs]
    specs = [VMEM] * len(outs)
    return pl.pallas_call(
        kernel,
        out_shape=shapes if len(outs) > 1 else shapes[0],
        in_specs=in_specs,
        out_specs=specs if len(outs) > 1 else specs[0],
        scratch_shapes=list(scratch),
        name=name,
        compiler_params=pltpu.CompilerParams(vmem_limit_bytes=48 * 1024 * 1024),
    )


def pack(cols, right_side, blocks, total_blocks):
    kernel = functools.partial(pack_kernel, total_blocks)
    return call(kernel, [(256, 256)], [SMEM, VMEM, VMEM], name="pack")(cols, right_side, blocks)


def basis(cols, own, pair, other):
    scratch = (pltpu.VMEM((256, 768), jnp.float32), pltpu.VMEM((6, 256, 128), jnp.float32))
    return call(basis_kernel, [(512, 128), (256, 512)], [SMEM, VMEM, VMEM, VMEM], scratch, name="basis")(cols, own, pair, other)


def total(parts, copies):
    kernel = functools.partial(total_kernel, copies)
    return call(kernel, [(copies,) + parts.shape[1:]], [VMEM], name="total")(parts)


def solve(sums, stack, right_side):
    return call(solve_kernel, [(64, 256), (64, 256)], [VMEM, VMEM, VMEM], name="solve")(sums, stack, right_side)


AXES = ("y", "z", "x", "core")
PLANE = ("y", "x", "core")


def shards(right_side, blocks, cols):
    devices = lax.axis_size(AXES)
    own = pack(cols, right_side, blocks, cols.shape[1] * devices)
    pair = lax.ppermute(own, AXES, [(i, i ^ 1) for i in range(devices)])
    other = lax.ppermute(own, AXES, [(i, ((i - 1) ^ 1) + 1 if i else devices - 1) if i < devices - 1 else (i, 0) for i in range(devices)])
    sums, stack = basis(cols, own, pair, other)
    parts = lax.all_to_all(sums.reshape(32, 16, 128), PLANE, 0, 0)
    parts = lax.all_to_all(total(parts, 16), "z", 0, 0)
    sums = lax.all_to_all(total(parts, 32), PLANE, 0, 0)
    return tuple(solve(sums.reshape(512, 128), stack, right_side))


def solution(mesh):
    grid = Mesh(mesh.devices.reshape(4, 16, 4, 2), AXES)
    in_specs = (P(None, AXES), P(None, None, AXES), P(None, AXES))
    out_specs = (P(None, AXES), P(None, AXES))
    return jax.shard_map(shards, mesh=grid, in_specs=in_specs, out_specs=out_specs, check_vma=False)
```

```python
import functools

import jax
import jax.numpy as jnp
from jax import lax
from jax.experimental import pallas as pl
from jax.experimental.pallas import tpu as pltpu
from jax.sharding import Mesh, PartitionSpec as P

SCALE = 1.25
S = 4
BS = 64
HIGH = lax.Precision.HIGHEST

HBM = pl.BlockSpec(memory_space=pltpu.HBM)
VMEM = pl.BlockSpec(memory_space=pltpu.VMEM)
SMEM = pl.BlockSpec(memory_space=pltpu.SMEM)


def dot(a, b, dims):
    return lax.dot_general(a, b, (dims, ((), ())), precision=HIGH, preferred_element_type=jnp.float32)


def pack_kernel(total_blocks, cols_ref, right_ref, blocks_ref, out_ref, part_ref, part_sem, right_sem):
    slots, _, width = part_ref.shape
    copies = [pltpu.make_async_copy(blocks_ref.at[slot], part_ref.at[slot], part_sem.at[slot]) for slot in range(slots)]
    for copy in copies:
        copy.start()
    last = pltpu.make_async_copy(right_ref, out_ref.at[192:256], right_sem)
    last.start()
    lane = lax.broadcasted_iota(jnp.int32, (1, width), 1) // BS
    offsets = []
    for slot in (5, 6):
        offset = jnp.zeros((1, width), jnp.int32)
        for row in range(width // BS):
            delta = cols_ref[row, slot] - cols_ref[row, 0]
            delta = jnp.where(delta > 1, delta - total_blocks, delta)
            delta = jnp.where(delta < -1, delta + total_blocks, delta)
            offset = jnp.where(lane == row, delta, offset)
        offsets.append(offset)
    for copy in copies:
        copy.wait()
    for at, value, fixed in ((0, -1, (2, 4)), (64, 0, (0,)), (128, 1, (1, 3))):
        kept = sum(part_ref[slot] for slot in fixed)
        for slot, offset in zip((5, 6), offsets):
            kept = kept + jnp.where(offset == value, part_ref[slot], 0.0)
        out_ref[at : at + 64, :] = kept
    last.wait()


def basis_kernel(cols_ref, own_ref, pair_ref, other_ref, sums_ref, stack_ref, ext_ref, band_ref):
    even = lax.rem(cols_ref[0, 0] // 4, 2) == 0

    @pl.when(even)
    def _():
        ext_ref[:, 0:256] = other_ref[...]
        ext_ref[:, 512:768] = pair_ref[...]

    @pl.when(jnp.logical_not(even))
    def _():
        ext_ref[:, 0:256] = pair_ref[...]
        ext_ref[:, 512:768] = other_ref[...]

    ext_ref[:, 256:512] = own_ref[...]
    left = lax.broadcasted_iota(jnp.int32, (BS, 128), 1) < BS
    for p in range(6):
        at = slice(128 * p, 128 * (p + 1))
        minus, zero, plus = ext_ref[0:64, at], ext_ref[64:128, at], ext_ref[128:192, at]
        band_ref[p, 0:64, :] = jnp.where(left, minus, 0.0)
        band_ref[p, 64:128, :] = jnp.where(left, zero, minus)
        band_ref[p, 128:192, :] = jnp.where(left, plus, zero)
        band_ref[p, 192:256, :] = jnp.where(left, 0.0, plus)
    current = ext_ref[192:256, :]
    first = 0
    own = [current[:, 256:512]]
    images = []
    for step, (low, high) in enumerate(((0, 6), (1, 5), (1, 5), (2, 4))):
        rolled = pltpu.roll(current, 64, 1)
        parts = []
        for p in range(low, high):
            at = 128 * (p - first)
            if at + 256 <= rolled.shape[1]:
                window = rolled[:, at : at + 256]
            else:
                window = jnp.concatenate([rolled[:, at:], rolled[:, :128]], axis=1)
            parts.append(dot(window, band_ref[p], ((1,), (0,))))
        product = jnp.concatenate(parts, axis=1)
        inner = product[:, 256 - 128 * low : 512 - 128 * low]
        images.append(own[step] + inner)
        current = SCALE * product
        first = low
        own.append(SCALE * inner)
    w = jnp.concatenate(images, axis=0)
    stack_ref[:, 0:256] = jnp.concatenate(own[:S], axis=0)
    stack_ref[:, 256:512] = w
    z = jnp.concatenate([w, own[0]], axis=0)
    g = [dot(images[k], z[64 * k :], ((1,), (1,))) for k in range(S)]
    sums_ref[0:64, :] = g[0][:, 0:128]
    sums_ref[64:128, :] = g[0][:, 128:256]
    sums_ref[128:192, :] = g[1][:, 0:128]
    sums_ref[192:256, :] = g[1][:, 128:256]
    sums_ref[256:320, :] = g[2][:, 0:128]
    sums_ref[320:384, :] = g[3]
    sums_ref[384:448, :] = jnp.concatenate([g[0][:, 256:320], g[2][:, 128:192]], axis=1)
    sums_ref[448:512, :] = jnp.zeros((64, 128), jnp.float32)


def total_kernel(copies, in_ref, out_ref):
    total = in_ref[0]
    for k in range(1, in_ref.shape[0]):
        total = total + in_ref[k]
    for k in range(copies):
        out_ref[k] = total


WINDOW = 3


def inverse_of(x):
    return 1.0 / x


def eliminate(part):
    groups, tiles = BS // 8, len(part[0])
    rows = lax.broadcasted_iota(jnp.int32, (8, 1), 0)
    scaled = [[None] * tiles for _ in range(groups)]

    def fetch(k, begin):
        return {g: jnp.broadcast_to(part[g][0][:, k : k + 1], (8, 128)) for g in range(begin, groups)}

    ahead = {k: fetch(k, 0) for k in range(2 * WINDOW)}
    for k in range(0, BS, 2):
        at, row = k // 8, k % 8
        first, second = ahead.pop(k), ahead.pop(k + 1)
        a, b, d = first[at][row : row + 1, :], first[at][row + 1 : row + 2, :], second[at][row + 1 : row + 2, :]
        inverse = inverse_of(a * d - b * b)
        p, q, r = d * inverse, -b * inverse, a * inverse

        def solved(top, low):
            n = top.shape[1]
            return p[:, :n] * top + q[:, :n] * low, q[:, :n] * top + r[:, :n] * low

        if row < 6:
            keep = rows > row + 1
            first[at], second[at] = jnp.where(keep, first[at], 0.0), jnp.where(keep, second[at], 0.0)
            live = range(at, groups)
        else:
            live = range(at + 1, groups)
        for column in ahead.values():
            top, low = solved(column[at][row : row + 1, :], column[at][row + 1 : row + 2, :])
            for g in live:
                if g in column:
                    column[g] = column[g] - (first[g] * top + second[g] * low)
        for t in range(tiles):
            top, low = solved(part[at][t][row : row + 1, :], part[at][t][row + 1 : row + 2, :])
            n = top.shape[1]
            for g in live:
                part[g][t] = part[g][t] - (first[g][:, :n] * top + second[g][:, :n] * low)
            pair = jnp.where(rows == row, top, low)
            scaled[at][t] = pair if row == 0 else jnp.where(rows < row, scaled[at][t], pair)
        for late in (k + 2 * WINDOW, k + 2 * WINDOW + 1):
            if late < BS:
                ahead[late] = fetch(late, (k + 2) // 8)
    join = lambda x: [jnp.concatenate([x[g][t] for g in range(groups)], axis=0) for t in range(tiles)]
    return join(part), join(scaled)


def solve_kernel(sums_ref, stack_ref, update_ref, residual_ref):
    u = [sums_ref[64 * k : 64 * (k + 1), :] for k in range(7)]
    row = lax.broadcasted_iota(jnp.int32, (BS, 128), 0)
    lane = lax.broadcasted_iota(jnp.int32, (BS, 128), 1)
    eye = jnp.where(row == lane % BS, 1.0, 0.0)
    left = lane < BS
    half = lambda tiles, i: tiles[i // 2][:, 64 * (i % 2) : 64 * (i % 2 + 1)]
    tiles = {
        0: [u[0], u[1], jnp.where(left, u[6], eye)],
        1: [u[2], u[3], eye[:, 0:64]],
        2: [u[4], jnp.where(left, eye, u[6])],
        3: [u[5], eye[:, 0:64]],
    }
    order = {0: (0, 1, 2, 3, 4, 5), 1: (1, 2, 3, 4, 5), 2: (2, 3, 5, 4), 3: (3, 4, 5)}
    solved = {}
    for k in range(S):
        part = [[t[8 * g : 8 * (g + 1), :] for t in tiles[k]] for g in range(BS // 8)]
        part, scaled = eliminate(part)
        y = {name: half(part, i) for i, name in enumerate(order[k])}
        z = {name: half(scaled, i) for i, name in enumerate(order[k])}
        for i in range(k + 1, S):
            names = [n for n in order[i] if n < 5]
            change = dot(y[i], jnp.concatenate([z[n] for n in names], axis=1), ((0,), (0,)))
            fresh = []
            for t, tile in enumerate(tiles[i]):
                have = order[i][2 * t : 2 * t + 2]
                cut = [change[:, 64 * names.index(n) : 64 * (names.index(n) + 1)] if n < 5 else jnp.zeros((BS, BS), jnp.float32) for n in have]
                whole = all(n < 5 for n in have)
                if whole:
                    fresh.append(tile - change[:, 64 * names.index(have[0]) : 64 * names.index(have[0]) + 64 * len(have)])
                elif any(n < 5 for n in have):
                    fresh.append(tile - jnp.concatenate(cut, axis=1))
                else:
                    fresh.append(tile)
            tiles[i] = fresh
        names = [n for n in range(k + 1, 5)]
        solved[k] = dot(y[5], jnp.concatenate([z[n] for n in names], axis=1), ((0,), (0,)))
    x = [None] * S
    both = None
    for k in range(S - 1, -1, -1):
        x[k] = solved[k][:, 64 * (S - 1 - k) : 64 * (S - k)]
        if k < S - 1:
            x[k] = x[k] - dot(solved[k][:, : 64 * (S - 1 - k)], jnp.concatenate(x[k + 1 :], axis=0), ((1,), (0,)))
        term = dot(x[k], stack_ref[64 * k : 64 * (k + 1), :], ((0,), (0,)))
        both = term if both is None else both + term
    update_ref[...] = both[:, 0:256]
    residual_ref[...] = stack_ref[0:64, 0:256] - both[:, 256:512]


def call(kernel, outs, in_specs, scratch=(), name=None):
    shapes = [jax.ShapeDtypeStruct(s, jnp.float32) for s in outs]
    specs = [VMEM] * len(outs)
    return pl.pallas_call(
        kernel,
        out_shape=shapes if len(outs) > 1 else shapes[0],
        in_specs=in_specs,
        out_specs=specs if len(outs) > 1 else specs[0],
        scratch_shapes=list(scratch),
        name=name,
        compiler_params=pltpu.CompilerParams(vmem_limit_bytes=48 * 1024 * 1024),
    )


def pack(cols, right_side, blocks, total_blocks):
    kernel = functools.partial(pack_kernel, total_blocks)
    scratch = (pltpu.VMEM(blocks.shape, jnp.float32), pltpu.SemaphoreType.DMA((blocks.shape[0],)), pltpu.SemaphoreType.DMA)
    return call(kernel, [(256, 256)], [SMEM, HBM, HBM], scratch, name="pack")(cols, *(pltpu.with_memory_space_constraint(a, pltpu.HBM) for a in (right_side, blocks)))


def basis(cols, own, pair, other):
    scratch = (pltpu.VMEM((256, 768), jnp.float32), pltpu.VMEM((6, 256, 128), jnp.float32))
    return call(basis_kernel, [(512, 128), (256, 512)], [SMEM, VMEM, VMEM, VMEM], scratch, name="basis")(cols, own, pair, other)


def total(parts, copies):
    kernel = functools.partial(total_kernel, copies)
    return call(kernel, [(copies,) + parts.shape[1:]], [VMEM], name="total")(parts)


def solve(sums, stack):
    return call(solve_kernel, [(64, 256), (64, 256)], [VMEM, VMEM], name="solve")(sums, stack)


AXES = ("y", "z", "x", "core")
PLANE = ("y", "x", "core")


def shards(right_side, blocks, cols):
    devices = lax.axis_size(AXES)
    cols = cols.T
    own = pack(cols, right_side, blocks, cols.shape[0] * devices)
    pair = lax.ppermute(own, AXES, [(i, i ^ 1) for i in range(devices)])
    other = lax.ppermute(own, AXES, [(i, ((i - 1) ^ 1) + 1 if i else devices - 1) if i < devices - 1 else (i, 0) for i in range(devices)])
    sums, stack = basis(cols, own, pair, other)
    parts = lax.all_to_all(sums.reshape(32, 16, 128), PLANE, 0, 0)
    parts = lax.all_to_all(total(parts, 16), "z", 0, 0)
    sums = lax.all_to_all(total(parts, 32), PLANE, 0, 0)
    return tuple(solve(sums.reshape(512, 128), stack))


def solution(mesh):
    grid = Mesh(mesh.devices.reshape(4, 16, 4, 2), AXES)
    in_specs = (P(None, AXES), P(None, None, AXES), P(None, AXES))
    out_specs = (P(None, AXES), P(None, AXES))
    return jax.shard_map(shards, mesh=grid, in_specs=in_specs, out_specs=out_specs, check_vma=False)
```

```python
import functools

import jax
import jax.numpy as jnp
from jax import lax
from jax.experimental import pallas as pl
from jax.experimental.pallas import tpu as pltpu
from jax.sharding import Mesh, PartitionSpec as P

SCALE = 1.25
S = 4
BS = 64

HBM = pl.BlockSpec(memory_space=pltpu.HBM)
VMEM = pl.BlockSpec(memory_space=pltpu.VMEM)
SMEM = pl.BlockSpec(memory_space=pltpu.SMEM)


def pack_kernel(total_blocks, cols_hbm, right_ref, blocks_ref, out_ref, flag_ref, cols_ref, part_ref, cols_sem, part_sem, right_sem):
    slots, _, width = part_ref.shape
    table = pltpu.make_async_copy(cols_hbm, cols_ref, cols_sem)
    table.start()
    copies = [pltpu.make_async_copy(blocks_ref.at[slot], part_ref.at[slot], part_sem.at[slot]) for slot in range(slots)]
    for copy in copies:
        copy.start()
    last = pltpu.make_async_copy(right_ref, out_ref.at[192:256], right_sem)
    last.start()
    lane = lax.broadcasted_iota(jnp.int32, (1, width), 1) // BS
    table.wait()
    odd = lax.rem(cols_ref[0, 0] // (width // BS), 2)
    flag_ref[...] = jnp.full(flag_ref.shape, 1 - odd, jnp.int32).astype(jnp.float32)
    offsets = []
    for slot in (5, 6):
        offset = jnp.zeros((1, width), jnp.int32)
        for row in range(width // BS):
            delta = cols_ref[row, slot] - cols_ref[row, 0]
            delta = jnp.where(delta > 1, delta - total_blocks, delta)
            delta = jnp.where(delta < -1, delta + total_blocks, delta)
            offset = jnp.where(lane == row, delta, offset)
        offsets.append(offset)
    for copy in copies:
        copy.wait()
    for at, value, fixed in ((0, -1, (2, 4)), (64, 0, (0,)), (128, 1, (1, 3))):
        kept = sum(part_ref[slot] for slot in fixed)
        for slot, offset in zip((5, 6), offsets):
            kept = kept + jnp.where(offset == value, part_ref[slot], 0.0)
        out_ref[at : at + 64, :] = kept
    last.wait()


def halves(a):
    high = a.astype(jnp.bfloat16)
    return high, (a - high.astype(jnp.float32)).astype(jnp.bfloat16)


def product(a, b, dims):
    one = lambda x, y: lax.dot_general(x, y, (dims, ((), ())), preferred_element_type=jnp.float32)
    return one(a[0], b[0]) + (one(a[0], b[1]) + one(a[1], b[0]))


def basis_kernel(flag_ref, own_ref, pair_ref, other_ref, sums_ref, stack_ref):
    even = flag_ref[0:1, :] > 0
    left = lax.broadcasted_iota(jnp.int32, (BS, 128), 1) < BS
    bands, tiles = [], []
    for p in range(6):
        at = slice(128 * (p % 2), 128 * (p % 2 + 1))
        if p < 2:
            get = lambda r: jnp.where(even, other_ref[r, at], pair_ref[r, at])
        elif p < 4:
            get = lambda r: own_ref[r, at]
        else:
            get = lambda r: jnp.where(even, pair_ref[r, at], other_ref[r, at])
        minus, zero, plus = get(slice(0, 64)), get(slice(64, 128)), get(slice(128, 192))
        band = jnp.concatenate(
            [
                jnp.where(left, minus, 0.0),
                jnp.where(left, zero, minus),
                jnp.where(left, plus, zero),
                jnp.where(left, 0.0, plus),
            ],
            axis=0,
        )
        bands.append(halves(SCALE * band))
        tiles.append(get(slice(192, 256)))
    own = [jnp.concatenate(tiles[2:4], axis=1)]
    first = 0
    for low, high in ((0, 6), (1, 5), (1, 5), (2, 4)):
        current = jnp.concatenate(tiles, axis=1)
        rolled = halves(pltpu.roll(current, 64, 1))
        fresh = []
        for p in range(low, high):
            at = 128 * (p - first)
            if at + 256 <= current.shape[1]:
                window = [r[:, at : at + 256] for r in rolled]
            else:
                window = [jnp.concatenate([r[:, at:], r[:, :128]], axis=1) for r in rolled]
            fresh.append(product(window, bands[p], ((1,), (0,))))
        own.append(jnp.concatenate(fresh[2 - low : 4 - low], axis=1))
        tiles = fresh
        first = low
    images = [own[k] + own[k + 1] / SCALE for k in range(S)]
    w = jnp.concatenate(images, axis=0)
    stack_ref[:, 0:256] = jnp.concatenate(own[:S], axis=0)
    stack_ref[:, 256:512] = w
    z = jnp.concatenate([w, own[0]], axis=0)
    z = halves(z)
    g = [product([h[64 * k : 64 * (k + 1)] for h in z], [h[64 * k :] for h in z], ((1,), (1,))) for k in range(S)]
    sums_ref[0:64, :] = g[0][:, 0:128]
    sums_ref[64:128, :] = g[0][:, 128:256]
    sums_ref[128:192, :] = g[1][:, 0:128]
    sums_ref[192:256, :] = g[1][:, 128:256]
    sums_ref[256:320, :] = g[2][:, 0:128]
    sums_ref[320:384, :] = g[3]
    sums_ref[384:448, :] = jnp.concatenate([g[0][:, 256:320], g[2][:, 128:192]], axis=1)
    sums_ref[448:512, :] = jnp.zeros((64, 128), jnp.float32)


def total_kernel(copies, in_ref, out_ref):
    total = in_ref[0]
    for k in range(1, in_ref.shape[0]):
        total = total + in_ref[k]
    for k in range(copies):
        out_ref[k] = total


WINDOW = 4


def narrow(a, b, dims):
    return product(halves(a), halves(b), dims)


def eliminate(part):
    groups, tiles = BS // 8, len(part[0])
    rows = lax.broadcasted_iota(jnp.int32, (8, 1), 0)
    scaled = [[None] * tiles for _ in range(groups)]

    def fetch(k, begin):
        return {g: jnp.broadcast_to(part[g][0][:, k : k + 1], (8, 128)) for g in range(begin, groups)}

    ahead = {k: fetch(k, 0) for k in range(2 * WINDOW)}
    for k in range(0, BS, 2):
        at, row = k // 8, k % 8
        first, second = ahead.pop(k), ahead.pop(k + 1)
        a, b, d = first[at][row : row + 1, :], first[at][row + 1 : row + 2, :], second[at][row + 1 : row + 2, :]
        inverse = 1.0 / (a * d - b * b)
        p, q, r = d * inverse, -b * inverse, a * inverse

        def solved(top, low):
            n = top.shape[1]
            return p[:, :n] * top + q[:, :n] * low, q[:, :n] * top + r[:, :n] * low

        if row < 6:
            keep = rows > row + 1
            first[at], second[at] = jnp.where(keep, first[at], 0.0), jnp.where(keep, second[at], 0.0)
            live = range(at, groups)
        else:
            live = range(at + 1, groups)
        for column in ahead.values():
            top, low = solved(column[at][row : row + 1, :], column[at][row + 1 : row + 2, :])
            for g in live:
                if g in column:
                    column[g] = column[g] - (first[g] * top + second[g] * low)
        for t in range(tiles):
            top, low = solved(part[at][t][row : row + 1, :], part[at][t][row + 1 : row + 2, :])
            n = top.shape[1]
            for g in live:
                part[g][t] = part[g][t] - (first[g][:, :n] * top + second[g][:, :n] * low)
            pair = jnp.where(rows == row, top, low)
            scaled[at][t] = pair if row == 0 else jnp.where(rows < row, scaled[at][t], pair)
        for late in (k + 2 * WINDOW, k + 2 * WINDOW + 1):
            if late < BS:
                ahead[late] = fetch(late, (k + 2) // 8)
    join = lambda x: [jnp.concatenate([x[g][t] for g in range(groups)], axis=0) for t in range(tiles)]
    return join(part), join(scaled)


def solve_kernel(sums_ref, stack_ref, update_ref, residual_ref):
    u = [sums_ref[64 * k : 64 * (k + 1), :] for k in range(7)]
    row = lax.broadcasted_iota(jnp.int32, (BS, 128), 0)
    lane = lax.broadcasted_iota(jnp.int32, (BS, 128), 1)
    eye = jnp.where(row == lane % BS, 1.0, 0.0)
    left = lane < BS
    half = lambda tiles, i: tiles[i // 2][:, 64 * (i % 2) : 64 * (i % 2 + 1)]
    tiles = {
        0: [u[0], u[1], jnp.where(left, u[6], eye)],
        1: [u[2], u[3], eye[:, 0:64]],
        2: [u[4], jnp.where(left, eye, u[6])],
        3: [u[5], eye[:, 0:64]],
    }
    order = {0: (0, 1, 2, 3, 4, 5), 1: (1, 2, 3, 4, 5), 2: (2, 3, 5, 4), 3: (3, 4, 5)}
    spans = [stack_ref[64 * k : 64 * (k + 1), :] for k in range(S)]
    both = None
    for k in range(S):
        part = [[t[8 * g : 8 * (g + 1), :] for t in tiles[k]] for g in range(BS // 8)]
        part, scaled = eliminate(part)
        y = {name: half(part, i) for i, name in enumerate(order[k])}
        z = {name: half(scaled, i) for i, name in enumerate(order[k])}
        for i in range(k + 1, S):
            names = [n for n in order[i] if n < 5]
            change = narrow(y[i], jnp.concatenate([z[n] for n in names], axis=1), ((0,), (0,)))
            fresh = []
            for t, tile in enumerate(tiles[i]):
                have = order[i][2 * t : 2 * t + 2]
                cut = [change[:, 64 * names.index(n) : 64 * (names.index(n) + 1)] if n < 5 else jnp.zeros((BS, BS), jnp.float32) for n in have]
                if all(n < 5 for n in have):
                    at = 64 * names.index(have[0])
                    fresh.append(tile - change[:, at : at + 64 * len(have)])
                elif any(n < 5 for n in have):
                    fresh.append(tile - jnp.concatenate(cut, axis=1))
                else:
                    fresh.append(tile)
            tiles[i] = fresh
        solved = narrow(y[5], jnp.concatenate([z[n] for n in range(k + 1, 5)], axis=1), ((0,), (0,)))
        term = narrow(solved[:, 64 * (S - 1 - k) :], spans[k], ((0,), (0,)))
        both = term if both is None else both + term
        for i in range(k + 1, S):
            spans[i] = spans[i] - narrow(solved[:, 64 * (i - k - 1) : 64 * (i - k)], spans[k], ((0,), (0,)))
    update_ref[...] = both[:, 0:256]
    residual_ref[...] = stack_ref[0:64, 0:256] - both[:, 256:512]


def call(kernel, outs, in_specs, scratch=(), name=None):
    shapes = [jax.ShapeDtypeStruct(s, jnp.float32) for s in outs]
    specs = [VMEM] * len(outs)
    return pl.pallas_call(
        kernel,
        out_shape=shapes if len(outs) > 1 else shapes[0],
        in_specs=in_specs,
        out_specs=specs if len(outs) > 1 else specs[0],
        scratch_shapes=list(scratch),
        name=name,
        compiler_params=pltpu.CompilerParams(vmem_limit_bytes=48 * 1024 * 1024),
    )


def pack(cols, right_side, blocks, total_blocks):
    kernel = functools.partial(pack_kernel, total_blocks)
    scratch = (
        pltpu.SMEM(cols.shape, jnp.int32),
        pltpu.VMEM(blocks.shape, jnp.float32),
        pltpu.SemaphoreType.DMA,
        pltpu.SemaphoreType.DMA((blocks.shape[0],)),
        pltpu.SemaphoreType.DMA,
    )
    arrays = [pltpu.with_memory_space_constraint(a, pltpu.HBM) for a in (cols, right_side, blocks)]
    return call(kernel, [(256, 256), (8, 128)], [HBM] * 3, scratch, name="pack")(*arrays)


def basis(flag, own, pair, other):
    return call(basis_kernel, [(512, 128), (256, 512)], [VMEM] * 4, name="basis")(flag, own, pair, other)


def total(parts, copies):
    kernel = functools.partial(total_kernel, copies)
    return call(kernel, [(copies,) + parts.shape[1:]], [VMEM], name="total")(parts)


def solve(sums, stack):
    return call(solve_kernel, [(64, 256), (64, 256)], [VMEM, VMEM], name="solve")(sums, stack)


AXES = ("y", "z", "x", "core")
PLANE = ("y", "x", "core")


def shards(right_side, blocks, cols):
    devices = lax.axis_size(AXES)
    cols = cols.T
    own, flag = pack(cols, right_side, blocks, cols.shape[0] * devices)
    pair = lax.ppermute(own, AXES, [(i, i ^ 1) for i in range(devices)])
    other = lax.ppermute(own, AXES, [(i, ((i - 1) ^ 1) + 1 if i else devices - 1) if i < devices - 1 else (i, 0) for i in range(devices)])
    sums, stack = basis(flag, own, pair, other)
    parts = lax.all_to_all(sums.reshape(32, 16, 128), PLANE, 0, 0)
    parts = lax.all_to_all(total(parts, 16), "z", 0, 0)
    sums = lax.all_to_all(total(parts, 32), PLANE, 0, 0)
    return tuple(solve(sums.reshape(512, 128), stack))


def solution(mesh):
    grid = Mesh(mesh.devices.reshape(4, 16, 4, 2), AXES)
    in_specs = (P(None, AXES), P(None, None, AXES), P(None, AXES))
    out_specs = (P(None, AXES), P(None, AXES))
    return jax.shard_map(shards, mesh=grid, in_specs=in_specs, out_specs=out_specs, check_vma=False)
```

```python
import functools

import jax
import jax.numpy as jnp
from jax import lax
from jax.experimental import pallas as pl
from jax.experimental.pallas import tpu as pltpu
from jax.sharding import Mesh, PartitionSpec as P

SCALE = 1.25
S = 4
BS = 64

HBM = pl.BlockSpec(memory_space=pltpu.HBM)
VMEM = pl.BlockSpec(memory_space=pltpu.VMEM)
SMEM = pl.BlockSpec(memory_space=pltpu.SMEM)


def halves(a):
    high = a.astype(jnp.bfloat16)
    return high, (a - high.astype(jnp.float32)).astype(jnp.bfloat16)


def product(a, b, dims):
    one = lambda x, y: lax.dot_general(x, y, (dims, ((), ())), preferred_element_type=jnp.float32)
    return one(a[0], b[0]) + (one(a[0], b[1]) + one(a[1], b[0]))


def banded(minus, zero, plus):
    left = lax.broadcasted_iota(jnp.int32, (BS, 128), 1) < BS
    parts = [
        jnp.where(left, minus, 0.0),
        jnp.where(left, zero, minus),
        jnp.where(left, plus, zero),
        jnp.where(left, 0.0, plus),
    ]
    return halves(SCALE * jnp.concatenate(parts, axis=0))


def pack_kernel(total_blocks, cols_hbm, right_ref, blocks_ref, out_ref, other_ref, pair_ref, flag_ref, cols_ref, part_ref, cols_sem, part_sem, right_sem):
    slots, _, width = part_ref.shape
    table = pltpu.make_async_copy(cols_hbm, cols_ref, cols_sem)
    table.start()
    copies = [pltpu.make_async_copy(blocks_ref.at[slot], part_ref.at[slot], part_sem.at[slot]) for slot in range(slots)]
    for copy in copies:
        copy.start()
    last = pltpu.make_async_copy(right_ref, out_ref.at[192:256], right_sem)
    last.start()
    lane = lax.broadcasted_iota(jnp.int32, (1, width), 1) // BS
    table.wait()
    odd = lax.rem(cols_ref[0, 0] // (width // BS), 2)
    flag_ref[...] = jnp.full(flag_ref.shape, 1 - odd, jnp.int32).astype(jnp.float32)
    offsets = []
    for slot in (5, 6):
        offset = jnp.zeros((1, width), jnp.int32)
        for row in range(width // BS):
            delta = cols_ref[row, slot] - cols_ref[row, 0]
            delta = jnp.where(delta > 1, delta - total_blocks, delta)
            delta = jnp.where(delta < -1, delta + total_blocks, delta)
            offset = jnp.where(lane == row, delta, offset)
        offsets.append(offset)
    for copy in copies:
        copy.wait()
    inner = []
    for at, value, fixed in ((0, -1, (2, 4)), (64, 0, (0,)), (128, 1, (1, 3))):
        kept = sum(part_ref[slot] for slot in fixed)
        for slot, offset in zip((5, 6), offsets):
            kept = kept + jnp.where(offset == value, part_ref[slot], 0.0)
        out_ref[at : at + 64, :] = kept
        inner.append(pltpu.roll(kept, 64, 1)[:, 128:256])
    last.wait()
    image = product(halves(out_ref[192:256, :]), banded(*inner), ((1,), (0,)))
    even = jnp.full((1, 128), odd, jnp.int32) == 0
    head, tail = out_ref[:, 0:128], out_ref[:, 128:256]
    pair_ref[0:256, :] = jnp.where(even, tail, head)
    other_ref[0:256, :] = jnp.where(even, head, tail)
    pair_ref[256:320, :] = image
    other_ref[256:320, :] = image


def basis_kernel(flag_ref, own_ref, other_ref, pair_ref, sums_ref, stack_ref):
    even = flag_ref[0:1, :] > 0
    pair, other = pair_ref[...], other_ref[...]
    ends = jnp.where(even, other, pair), jnp.where(even, pair, other)
    parts = [ends[0], own_ref[:, 0:128], own_ref[:, 128:256], ends[1]]
    bands = [banded(part[0:64], part[64:128], part[128:192]) for part in parts]
    edges = [halves(end[256:320]) for end in ends]

    def rolled(tiles):
        both = halves(pltpu.roll(jnp.concatenate(tiles, axis=1), 64, 1))
        shifted = [tuple(r[:, 128 * p : 128 * (p + 1)] for r in both) for p in range(4)]
        return shifted + shifted[:1]

    tiles = [part[192:256] for part in parts]
    own = [jnp.concatenate(tiles[1:3], axis=1)]
    for step in range(S):
        shifted = rolled(tiles)
        if step == 1:
            shifted[0], shifted[4] = edges
        fresh = list(tiles)
        for p in range(4) if step < S - 1 else (1, 2):
            window = [jnp.concatenate([a, b], axis=1) for a, b in zip(shifted[p], shifted[p + 1])]
            fresh[p] = product(window, bands[p], ((1,), (0,)))
        tiles = fresh
        own.append(jnp.concatenate(tiles[1:3], axis=1))
    images = [own[k] + own[k + 1] / SCALE for k in range(S)]
    w = jnp.concatenate(images, axis=0)
    stack_ref[:, 0:256] = jnp.concatenate(own[:S], axis=0)
    stack_ref[:, 256:512] = w
    z = jnp.concatenate([w, own[0]], axis=0)
    z = halves(z)
    g = [product([h[64 * k : 64 * (k + 1)] for h in z], [h[64 * k :] for h in z], ((1,), (1,))) for k in range(S)]
    sums_ref[0:64, :] = g[0][:, 0:128]
    sums_ref[64:128, :] = g[0][:, 128:256]
    sums_ref[128:192, :] = g[1][:, 0:128]
    sums_ref[192:256, :] = g[1][:, 128:256]
    sums_ref[256:320, :] = g[2][:, 0:128]
    sums_ref[320:384, :] = g[3]
    sums_ref[384:448, :] = jnp.concatenate([g[0][:, 256:320], g[2][:, 128:192]], axis=1)
    sums_ref[448:512, :] = jnp.zeros((64, 128), jnp.float32)


def total_kernel(copies, in_ref, out_ref):
    total = in_ref[0]
    for k in range(1, in_ref.shape[0]):
        total = total + in_ref[k]
    for k in range(copies):
        out_ref[k] = total


WINDOW = 4


def narrow(a, b, dims):
    return product(halves(a), halves(b), dims)


def eliminate(part):
    groups, tiles = BS // 8, len(part[0])
    rows = lax.broadcasted_iota(jnp.int32, (8, 1), 0)
    scaled = [[None] * tiles for _ in range(groups)]

    def fetch(k, begin):
        return {g: jnp.broadcast_to(part[g][0][:, k : k + 1], (8, 128)) for g in range(begin, groups)}

    ahead = {k: fetch(k, 0) for k in range(2 * WINDOW)}
    for k in range(0, BS, 2):
        at, row = k // 8, k % 8
        first, second = ahead.pop(k), ahead.pop(k + 1)
        a, b, d = first[at][row : row + 1, :], first[at][row + 1 : row + 2, :], second[at][row + 1 : row + 2, :]
        inverse = 1.0 / (a * d - b * b)
        p, q, r = d * inverse, -b * inverse, a * inverse

        def solved(top, low):
            n = top.shape[1]
            return p[:, :n] * top + q[:, :n] * low, q[:, :n] * top + r[:, :n] * low

        if row < 6:
            keep = rows > row + 1
            first[at], second[at] = jnp.where(keep, first[at], 0.0), jnp.where(keep, second[at], 0.0)
            live = range(at, groups)
        else:
            live = range(at + 1, groups)
        for column in ahead.values():
            top, low = solved(column[at][row : row + 1, :], column[at][row + 1 : row + 2, :])
            for g in live:
                if g in column:
                    column[g] = column[g] - (first[g] * top + second[g] * low)
        for t in range(tiles):
            top, low = solved(part[at][t][row : row + 1, :], part[at][t][row + 1 : row + 2, :])
            n = top.shape[1]
            for g in live:
                part[g][t] = part[g][t] - (first[g][:, :n] * top + second[g][:, :n] * low)
            pair = jnp.where(rows == row, top, low)
            scaled[at][t] = pair if row == 0 else jnp.where(rows < row, scaled[at][t], pair)
        for late in (k + 2 * WINDOW, k + 2 * WINDOW + 1):
            if late < BS:
                ahead[late] = fetch(late, (k + 2) // 8)
    join = lambda x: [jnp.concatenate([x[g][t] for g in range(groups)], axis=0) for t in range(tiles)]
    return join(part), join(scaled)


def solve_kernel(sums_ref, stack_ref, update_ref, residual_ref):
    u = [sums_ref[64 * k : 64 * (k + 1), :] for k in range(7)]
    row = lax.broadcasted_iota(jnp.int32, (BS, 128), 0)
    lane = lax.broadcasted_iota(jnp.int32, (BS, 128), 1)
    eye = jnp.where(row == lane % BS, 1.0, 0.0)
    left = lane < BS
    half = lambda tiles, i: tiles[i // 2][:, 64 * (i % 2) : 64 * (i % 2 + 1)]
    tiles = {
        0: [u[0], u[1], jnp.where(left, u[6], eye)],
        1: [u[2], u[3], eye[:, 0:64]],
        2: [u[4], jnp.where(left, eye, u[6])],
        3: [u[5], eye[:, 0:64]],
    }
    order = {0: (0, 1, 2, 3, 4, 5), 1: (1, 2, 3, 4, 5), 2: (2, 3, 5, 4), 3: (3, 4, 5)}
    spans = [stack_ref[64 * k : 64 * (k + 1), :] for k in range(S)]
    both = None
    for k in range(S):
        part = [[t[8 * g : 8 * (g + 1), :] for t in tiles[k]] for g in range(BS // 8)]
        part, scaled = eliminate(part)
        y = {name: half(part, i) for i, name in enumerate(order[k])}
        z = {name: half(scaled, i) for i, name in enumerate(order[k])}
        for i in range(k + 1, S):
            names = [n for n in order[i] if n < 5]
            change = narrow(y[i], jnp.concatenate([z[n] for n in names], axis=1), ((0,), (0,)))
            fresh = []
            for t, tile in enumerate(tiles[i]):
                have = order[i][2 * t : 2 * t + 2]
                cut = [change[:, 64 * names.index(n) : 64 * (names.index(n) + 1)] if n < 5 else jnp.zeros((BS, BS), jnp.float32) for n in have]
                if all(n < 5 for n in have):
                    at = 64 * names.index(have[0])
                    fresh.append(tile - change[:, at : at + 64 * len(have)])
                elif any(n < 5 for n in have):
                    fresh.append(tile - jnp.concatenate(cut, axis=1))
                else:
                    fresh.append(tile)
            tiles[i] = fresh
        solved = narrow(y[5], jnp.concatenate([z[n] for n in range(k + 1, 5)], axis=1), ((0,), (0,)))
        term = narrow(solved[:, 64 * (S - 1 - k) :], spans[k], ((0,), (0,)))
        both = term if both is None else both + term
        for i in range(k + 1, S):
            spans[i] = spans[i] - narrow(solved[:, 64 * (i - k - 1) : 64 * (i - k)], spans[k], ((0,), (0,)))
    update_ref[...] = both[:, 0:256]
    residual_ref[...] = stack_ref[0:64, 0:256] - both[:, 256:512]


def call(kernel, outs, in_specs, scratch=(), name=None):
    shapes = [jax.ShapeDtypeStruct(s, jnp.float32) for s in outs]
    specs = [VMEM] * len(outs)
    return pl.pallas_call(
        kernel,
        out_shape=shapes if len(outs) > 1 else shapes[0],
        in_specs=in_specs,
        out_specs=specs if len(outs) > 1 else specs[0],
        scratch_shapes=list(scratch),
        name=name,
        compiler_params=pltpu.CompilerParams(vmem_limit_bytes=48 * 1024 * 1024),
    )


def pack(cols, right_side, blocks, total_blocks):
    kernel = functools.partial(pack_kernel, total_blocks)
    scratch = (
        pltpu.SMEM(cols.shape, jnp.int32),
        pltpu.VMEM(blocks.shape, jnp.float32),
        pltpu.SemaphoreType.DMA,
        pltpu.SemaphoreType.DMA((blocks.shape[0],)),
        pltpu.SemaphoreType.DMA,
    )
    arrays = [pltpu.with_memory_space_constraint(a, pltpu.HBM) for a in (cols, right_side, blocks)]
    return call(kernel, [(256, 256), (320, 128), (320, 128), (8, 128)], [HBM] * 3, scratch, name="pack")(*arrays)


def basis(flag, own, other, pair):
    return call(basis_kernel, [(512, 128), (256, 512)], [VMEM] * 4, name="basis")(flag, own, other, pair)


def total(parts, copies):
    kernel = functools.partial(total_kernel, copies)
    return call(kernel, [(copies,) + parts.shape[1:]], [VMEM], name="total")(parts)


def solve(sums, stack):
    return call(solve_kernel, [(64, 256), (64, 256)], [VMEM, VMEM], name="solve")(sums, stack)


AXES = ("y", "z", "x", "core")
PLANE = ("y", "x", "core")


def shards(right_side, blocks, cols):
    devices = lax.axis_size(AXES)
    cols = cols.T
    own, other, pair, flag = pack(cols, right_side, blocks, cols.shape[0] * devices)
    other = lax.ppermute(other, AXES, [(i, ((i - 1) ^ 1) + 1) if 0 < i < devices - 1 else (i, devices - 1 - i) for i in range(devices)])
    pair = lax.ppermute(pair, AXES, [(i, i ^ 1) for i in range(devices)])
    sums, stack = basis(flag, own, other, pair)
    parts = lax.all_to_all(sums.reshape(32, 16, 128), PLANE, 0, 0)
    parts = lax.all_to_all(total(parts, 16), "z", 0, 0)
    sums = lax.all_to_all(total(parts, 32), PLANE, 0, 0)
    return tuple(solve(sums.reshape(512, 128), stack))


def solution(mesh):
    grid = Mesh(mesh.devices.reshape(4, 16, 4, 2), AXES)
    in_specs = (P(None, AXES), P(None, None, AXES), P(None, AXES))
    out_specs = (P(None, AXES), P(None, AXES))
    return jax.shard_map(shards, mesh=grid, in_specs=in_specs, out_specs=out_specs, check_vma=False)
```

```python
import functools

import jax
import jax.numpy as jnp
from jax import lax
from jax.experimental import pallas as pl
from jax.experimental.pallas import tpu as pltpu
from jax.sharding import Mesh, PartitionSpec as P

SCALE = 1.25
S = 4
BS = 64

HBM = pl.BlockSpec(memory_space=pltpu.HBM)
VMEM = pl.BlockSpec(memory_space=pltpu.VMEM)
SMEM = pl.BlockSpec(memory_space=pltpu.SMEM)


def halves(a):
    high = a.astype(jnp.bfloat16)
    return high, (a - high.astype(jnp.float32)).astype(jnp.bfloat16)


def product(a, b, dims):
    one = lambda x, y: lax.dot_general(x, y, (dims, ((), ())), preferred_element_type=jnp.float32)
    return one(a[0], b[0]) + (one(a[0], b[1]) + one(a[1], b[0]))


def banded(minus, zero, plus):
    left = lax.broadcasted_iota(jnp.int32, (BS, 128), 1) < BS
    parts = [
        jnp.where(left, minus, 0.0),
        jnp.where(left, zero, minus),
        jnp.where(left, plus, zero),
        jnp.where(left, 0.0, plus),
    ]
    return halves(SCALE * jnp.concatenate(parts, axis=0))


def pack_kernel(total_blocks, cols_hbm, right_ref, blocks_ref, out_ref, other_ref, pair_ref, flag_ref, cols_ref, part_ref, cols_sem, part_sem, right_sem):
    slots, _, width = part_ref.shape
    table = pltpu.make_async_copy(cols_hbm, cols_ref, cols_sem)
    table.start()
    copies = [pltpu.make_async_copy(blocks_ref.at[slot], part_ref.at[slot], part_sem.at[slot]) for slot in range(slots)]
    for copy in copies:
        copy.start()
    last = pltpu.make_async_copy(right_ref, out_ref.at[192:256], right_sem)
    last.start()
    lane = lax.broadcasted_iota(jnp.int32, (1, width), 1) // BS
    table.wait()
    odd = lax.rem(cols_ref[0, 0] // (width // BS), 2)
    flag_ref[...] = jnp.full(flag_ref.shape, 1 - odd, jnp.int32).astype(jnp.float32)
    offsets = []
    for slot in (5, 6):
        offset = jnp.zeros((1, width), jnp.int32)
        for row in range(width // BS):
            delta = cols_ref[row, slot] - cols_ref[row, 0]
            delta = jnp.where(delta > 1, delta - total_blocks, delta)
            delta = jnp.where(delta < -1, delta + total_blocks, delta)
            offset = jnp.where(lane == row, delta, offset)
        offsets.append(offset)
    for copy in copies:
        copy.wait()
    inner = []
    for at, value, fixed in ((0, -1, (2, 4)), (64, 0, (0,)), (128, 1, (1, 3))):
        kept = sum(part_ref[slot] for slot in fixed)
        for slot, offset in zip((5, 6), offsets):
            kept = kept + jnp.where(offset == value, part_ref[slot], 0.0)
        out_ref[at : at + 64, :] = kept
        inner.append(pltpu.roll(kept, 64, 1)[:, 128:256])
    last.wait()
    image = product(halves(out_ref[192:256, :]), banded(*inner), ((1,), (0,)))
    even = jnp.full((1, 128), odd, jnp.int32) == 0
    head, tail = out_ref[:, 0:128], out_ref[:, 128:256]
    pair_ref[0:256, :] = jnp.where(even, tail, head)
    other_ref[0:256, :] = jnp.where(even, head, tail)
    pair_ref[256:320, :] = image
    other_ref[256:320, :] = image


def basis_kernel(flag_ref, own_ref, other_ref, pair_ref, sums_ref, stack_ref):
    even = flag_ref[0:1, :] > 0
    pair, other = pair_ref[...], other_ref[...]
    ends = jnp.where(even, other, pair), jnp.where(even, pair, other)
    parts = [ends[0], own_ref[:, 0:128], own_ref[:, 128:256], ends[1]]
    bands = [banded(part[0:64], part[64:128], part[128:192]) for part in parts]
    edges = [halves(end[256:320]) for end in ends]

    def rolled(tiles):
        both = halves(pltpu.roll(jnp.concatenate(tiles, axis=1), 64, 1))
        shifted = [tuple(r[:, 128 * p : 128 * (p + 1)] for r in both) for p in range(4)]
        return shifted + shifted[:1]

    tiles = [part[192:256] for part in parts]
    own = [jnp.concatenate(tiles[1:3], axis=1)]
    for step in range(S):
        shifted = rolled(tiles)
        if step == 1:
            shifted[0], shifted[4] = edges
        fresh = list(tiles)
        for p in range(4) if step < S - 1 else (1, 2):
            window = [jnp.concatenate([a, b], axis=1) for a, b in zip(shifted[p], shifted[p + 1])]
            fresh[p] = product(window, bands[p], ((1,), (0,)))
        tiles = fresh
        own.append(jnp.concatenate(tiles[1:3], axis=1))
    images = [own[k] + own[k + 1] / SCALE for k in range(S)]
    w = jnp.concatenate(images, axis=0)
    stack_ref[:, 0:256] = jnp.concatenate(own[:S], axis=0)
    stack_ref[:, 256:512] = w
    z = jnp.concatenate([w, own[0]], axis=0)
    z = halves(z)
    g = [product([h[64 * k : 64 * (k + 1)] for h in z], [h[64 * k :] for h in z], ((1,), (1,))) for k in range(S)]
    sums_ref[0:64, :] = g[0][:, 0:128]
    sums_ref[64:128, :] = g[0][:, 128:256]
    sums_ref[128:192, :] = g[1][:, 0:128]
    sums_ref[192:256, :] = g[1][:, 128:256]
    sums_ref[256:320, :] = g[2][:, 0:128]
    sums_ref[320:384, :] = g[3]
    sums_ref[384:448, :] = jnp.concatenate([g[0][:, 256:320], g[2][:, 128:192]], axis=1)
    sums_ref[448:512, :] = jnp.zeros((64, 128), jnp.float32)


def total_kernel(copies, in_ref, out_ref):
    total = in_ref[0]
    for k in range(1, in_ref.shape[0]):
        total = total + in_ref[k]
    for k in range(copies):
        out_ref[k] = total


WINDOW = 4


def narrow(a, b, dims):
    return product(halves(a), halves(b), dims)


def eliminate(part):
    groups, tiles = BS // 8, len(part[0])
    rows = lax.broadcasted_iota(jnp.int32, (8, 1), 0)
    scaled = [[None] * tiles for _ in range(groups)]

    def fetch(k, begin):
        return {g: jnp.broadcast_to(part[g][0][:, k : k + 1], (8, 128)) for g in range(begin, groups)}

    ahead = {k: fetch(k, 0) for k in range(2 * WINDOW)}
    for k in range(0, BS, 2):
        at, row = k // 8, k % 8
        first, second = ahead.pop(k), ahead.pop(k + 1)
        up = lambda x: pltpu.roll(x, 7, 0)
        a, b, d = first[at], second[at], up(second[at])
        inverse = 1.0 / (a * d - b * b)
        p, q, r = (x[row : row + 1, :] for x in (d * inverse, b * inverse, a * inverse))

        def solved(x):
            n = x.shape[1]
            low, x = up(x)[row : row + 1, :], x[row : row + 1, :]
            top, low = p[:, :n] * x - q[:, :n] * low, r[:, :n] * low - q[:, :n] * x
            return top, low

        if row < 6:
            keep = rows > row + 1
            first[at], second[at] = jnp.where(keep, first[at], 0.0), jnp.where(keep, second[at], 0.0)
            live = range(at, groups)
        else:
            live = range(at + 1, groups)
        for column in ahead.values():
            top, low = solved(column[at])
            for g in live:
                if g in column:
                    column[g] = column[g] - (first[g] * top + second[g] * low)
        for t in range(tiles):
            top, low = solved(part[at][t])
            n = top.shape[1]
            for g in live:
                part[g][t] = part[g][t] - (first[g][:, :n] * top + second[g][:, :n] * low)
            pair = jnp.where(rows == row, top, low)
            scaled[at][t] = pair if row == 0 else jnp.where(rows < row, scaled[at][t], pair)
        for late in (k + 2 * WINDOW, k + 2 * WINDOW + 1):
            if late < BS:
                ahead[late] = fetch(late, (k + 2) // 8)
    join = lambda x: [jnp.concatenate([x[g][t] for g in range(groups)], axis=0) for t in range(tiles)]
    return join(part), join(scaled)


def solve_kernel(sums_ref, stack_ref, update_hbm, residual_hbm, update_ref, residual_ref, update_sem, residual_sem):
    u = [sums_ref[64 * k : 64 * (k + 1), :] for k in range(7)]
    row = lax.broadcasted_iota(jnp.int32, (BS, 128), 0)
    lane = lax.broadcasted_iota(jnp.int32, (BS, 128), 1)
    eye = jnp.where(row == lane % BS, 1.0, 0.0)
    left = lane < BS
    half = lambda tiles, i: tiles[i // 2][:, 64 * (i % 2) : 64 * (i % 2 + 1)]
    tiles = {
        0: [u[0], u[1], jnp.where(left, u[6], eye)],
        1: [u[2], u[3], eye[:, 0:64]],
        2: [u[4], jnp.where(left, eye, u[6])],
        3: [u[5], eye[:, 0:64]],
    }
    order = {0: (0, 1, 2, 3, 4, 5), 1: (1, 2, 3, 4, 5), 2: (2, 3, 5, 4), 3: (3, 4, 5)}
    spans = [stack_ref[64 * k : 64 * (k + 1), :] for k in range(S)]
    both = None
    for k in range(S):
        part = [[t[8 * g : 8 * (g + 1), :] for t in tiles[k]] for g in range(BS // 8)]
        part, scaled = eliminate(part)
        y = {name: half(part, i) for i, name in enumerate(order[k])}
        z = {name: half(scaled, i) for i, name in enumerate(order[k])}
        for i in range(k + 1, S):
            names = [n for n in order[i] if n < 5]
            change = narrow(y[i], jnp.concatenate([z[n] for n in names], axis=1), ((0,), (0,)))
            fresh = []
            for t, tile in enumerate(tiles[i]):
                have = order[i][2 * t : 2 * t + 2]
                cut = [change[:, 64 * names.index(n) : 64 * (names.index(n) + 1)] if n < 5 else jnp.zeros((BS, BS), jnp.float32) for n in have]
                if all(n < 5 for n in have):
                    at = 64 * names.index(have[0])
                    fresh.append(tile - change[:, at : at + 64 * len(have)])
                elif any(n < 5 for n in have):
                    fresh.append(tile - jnp.concatenate(cut, axis=1))
                else:
                    fresh.append(tile)
            tiles[i] = fresh
        solved = narrow(y[5], jnp.concatenate([z[n] for n in range(k + 1, 5)], axis=1), ((0,), (0,)))
        term = [narrow(solved[:, 64 * (S - 1 - k) :], spans[k][:, 256 * h : 256 * (h + 1)], ((0,), (0,))) for h in (0, 1)]
        both = term if both is None else [b + t for b, t in zip(both, term)]
        for i in range(k + 1, S):
            spans[i] = spans[i] - narrow(solved[:, 64 * (i - k - 1) : 64 * (i - k)], spans[k], ((0,), (0,)))
    update_ref[...] = both[0]
    update = pltpu.make_async_copy(update_ref, update_hbm, update_sem)
    update.start()
    residual_ref[...] = stack_ref[0:64, 0:256] - both[1]
    residual = pltpu.make_async_copy(residual_ref, residual_hbm, residual_sem)
    residual.start()
    update.wait()
    residual.wait()


def call(kernel, outs, in_specs, scratch=(), name=None, space=VMEM):
    shapes = [jax.ShapeDtypeStruct(s, jnp.float32) for s in outs]
    specs = [space] * len(outs)
    return pl.pallas_call(
        kernel,
        out_shape=shapes if len(outs) > 1 else shapes[0],
        in_specs=in_specs,
        out_specs=specs if len(outs) > 1 else specs[0],
        scratch_shapes=list(scratch),
        name=name,
        compiler_params=pltpu.CompilerParams(vmem_limit_bytes=48 * 1024 * 1024),
    )


def pack(cols, right_side, blocks, total_blocks):
    kernel = functools.partial(pack_kernel, total_blocks)
    scratch = (
        pltpu.SMEM(cols.shape, jnp.int32),
        pltpu.VMEM(blocks.shape, jnp.float32),
        pltpu.SemaphoreType.DMA,
        pltpu.SemaphoreType.DMA((blocks.shape[0],)),
        pltpu.SemaphoreType.DMA,
    )
    arrays = [pltpu.with_memory_space_constraint(a, pltpu.HBM) for a in (cols, right_side, blocks)]
    return call(kernel, [(256, 256), (320, 128), (320, 128), (8, 128)], [HBM] * 3, scratch, name="pack")(*arrays)


def basis(flag, own, other, pair):
    return call(basis_kernel, [(512, 128), (256, 512)], [VMEM] * 4, name="basis")(flag, own, other, pair)


def total(parts, copies):
    kernel = functools.partial(total_kernel, copies)
    return call(kernel, [(copies,) + parts.shape[1:]], [VMEM], name="total")(parts)


def solve(sums, stack):
    scratch = [pltpu.VMEM((64, 256), jnp.float32)] * 2 + [pltpu.SemaphoreType.DMA] * 2
    return call(solve_kernel, [(64, 256), (64, 256)], [VMEM, VMEM], scratch, "solve", HBM)(sums, stack)


AXES = ("y", "z", "x", "core")
PLANE = ("y", "x", "core")


def shards(right_side, blocks, cols):
    devices = lax.axis_size(AXES)
    cols = cols.T
    own, other, pair, flag = pack(cols, right_side, blocks, cols.shape[0] * devices)
    other = lax.ppermute(other, AXES, [(i, ((i - 1) ^ 1) + 1) if 0 < i < devices - 1 else (i, devices - 1 - i) for i in range(devices)])
    pair = lax.ppermute(pair, AXES, [(i, i ^ 1) for i in range(devices)])
    sums, stack = basis(flag, own, other, pair)
    parts = lax.all_to_all(sums.reshape(32, 16, 128), PLANE, 0, 0)
    parts = lax.all_to_all(total(parts, 16), "z", 0, 0)
    sums = lax.all_to_all(total(parts, 32), PLANE, 0, 0)
    return tuple(solve(sums.reshape(512, 128), stack))


def solution(mesh):
    grid = Mesh(mesh.devices.reshape(4, 16, 4, 2), AXES)
    in_specs = (P(None, AXES), P(None, None, AXES), P(None, AXES))
    out_specs = (P(None, AXES), P(None, AXES))
    return jax.shard_map(shards, mesh=grid, in_specs=in_specs, out_specs=out_specs, check_vma=False)
```

```python
import functools

import jax
import jax.numpy as jnp
from jax import lax
from jax.experimental import pallas as pl
from jax.experimental.pallas import tpu as pltpu
from jax.sharding import Mesh, PartitionSpec as P

SCALE = 1.25
S = 4
BS = 64

HBM = pl.BlockSpec(memory_space=pltpu.HBM)
VMEM = pl.BlockSpec(memory_space=pltpu.VMEM)
SMEM = pl.BlockSpec(memory_space=pltpu.SMEM)


def halves(a):
    high = a.astype(jnp.bfloat16)
    return high, (a - high.astype(jnp.float32)).astype(jnp.bfloat16)


def product(a, b, dims):
    one = lambda x, y: lax.dot_general(x, y, (dims, ((), ())), preferred_element_type=jnp.float32)
    return one(a[0], b[0]) + (one(a[0], b[1]) + one(a[1], b[0]))


def banded(minus, zero, plus):
    left = lax.broadcasted_iota(jnp.int32, (BS, 128), 1) < BS
    parts = [
        jnp.where(left, minus, 0.0),
        jnp.where(left, zero, minus),
        jnp.where(left, plus, zero),
        jnp.where(left, 0.0, plus),
    ]
    return halves(SCALE * jnp.concatenate(parts, axis=0))


def pack_kernel(total_blocks, cols_hbm, right_ref, blocks_ref, out_ref, other_ref, pair_ref, flag_ref, cols_ref, part_ref, cols_sem, part_sem, right_sem):
    slots, _, width = part_ref.shape
    table = pltpu.make_async_copy(cols_hbm, cols_ref, cols_sem)
    table.start()
    copies = [pltpu.make_async_copy(blocks_ref.at[slot], part_ref.at[slot], part_sem.at[slot]) for slot in range(slots)]
    for copy in copies:
        copy.start()
    last = pltpu.make_async_copy(right_ref, out_ref.at[192:256], right_sem)
    last.start()
    lane = lax.broadcasted_iota(jnp.int32, (1, width), 1) // BS
    table.wait()
    odd = lax.rem(cols_ref[0, 0] // (width // BS), 2)
    flag_ref[...] = jnp.full(flag_ref.shape, 1 - odd, jnp.int32).astype(jnp.float32)
    offsets = []
    for slot in (5, 6):
        offset = jnp.zeros((1, width), jnp.int32)
        for row in range(width // BS):
            delta = cols_ref[row, slot] - cols_ref[row, 0]
            delta = jnp.where(delta > 1, delta - total_blocks, delta)
            delta = jnp.where(delta < -1, delta + total_blocks, delta)
            offset = jnp.where(lane == row, delta, offset)
        offsets.append(offset)
    for copy in copies:
        copy.wait()
    inner = []
    for at, value, fixed in ((0, -1, (2, 4)), (64, 0, (0,)), (128, 1, (1, 3))):
        kept = sum(part_ref[slot] for slot in fixed)
        for slot, offset in zip((5, 6), offsets):
            kept = kept + jnp.where(offset == value, part_ref[slot], 0.0)
        out_ref[at : at + 64, :] = kept
        inner.append(pltpu.roll(kept, 64, 1)[:, 128:256])
    last.wait()
    image = product(halves(out_ref[192:256, :]), banded(*inner), ((1,), (0,)))
    even = jnp.full((1, 128), odd, jnp.int32) == 0
    head, tail = out_ref[:, 0:128], out_ref[:, 128:256]
    pair_ref[0:256, :] = jnp.where(even, tail, head)
    other_ref[0:256, :] = jnp.where(even, head, tail)
    pair_ref[256:320, :] = image
    other_ref[256:320, :] = image


def basis_kernel(flag_ref, own_ref, other_ref, pair_ref, sums_ref, stack_ref):
    even = flag_ref[0:1, :] > 0
    pair, other = pair_ref[...], other_ref[...]
    ends = jnp.where(even, other, pair), jnp.where(even, pair, other)
    parts = [ends[0], own_ref[:, 0:128], own_ref[:, 128:256], ends[1]]
    bands = [banded(part[0:64], part[64:128], part[128:192]) for part in parts]
    edges = [halves(end[256:320]) for end in ends]

    def rolled(tiles):
        both = halves(pltpu.roll(jnp.concatenate(tiles, axis=1), 64, 1))
        shifted = [tuple(r[:, 128 * p : 128 * (p + 1)] for r in both) for p in range(4)]
        return shifted + shifted[:1]

    tiles = [part[192:256] for part in parts]
    own = [jnp.concatenate(tiles[1:3], axis=1)]
    for step in range(S):
        shifted = rolled(tiles)
        if step == 1:
            shifted[0], shifted[4] = edges
        fresh = list(tiles)
        for p in range(4) if step < S - 1 else (1, 2):
            window = [jnp.concatenate([a, b], axis=1) for a, b in zip(shifted[p], shifted[p + 1])]
            fresh[p] = product(window, bands[p], ((1,), (0,)))
        tiles = fresh
        own.append(jnp.concatenate(tiles[1:3], axis=1))
    images = [own[k] + own[k + 1] / SCALE for k in range(S)]
    w = jnp.concatenate(images, axis=0)
    stack_ref[:, 0:256] = jnp.concatenate(own[:S], axis=0)
    stack_ref[:, 256:512] = w
    z = jnp.concatenate([w, own[0]], axis=0)
    z = halves(z)
    g = [product([h[64 * k : 64 * (k + 1)] for h in z], [h[64 * k :] for h in z], ((1,), (1,))) for k in range(S)]
    sums_ref[0:64, :] = g[0][:, 0:128]
    sums_ref[64:128, :] = g[0][:, 128:256]
    sums_ref[128:192, :] = g[1][:, 0:128]
    sums_ref[192:256, :] = g[1][:, 128:256]
    sums_ref[256:320, :] = g[2][:, 0:128]
    sums_ref[320:384, :] = g[3]
    sums_ref[384:448, :] = jnp.concatenate([g[0][:, 256:320], g[2][:, 128:192]], axis=1)
    sums_ref[448:512, :] = jnp.zeros((64, 128), jnp.float32)


def total_kernel(copies, in_ref, out_ref):
    total = in_ref[0]
    for k in range(1, in_ref.shape[0]):
        total = total + in_ref[k]
    for k in range(copies):
        out_ref[k] = total


WINDOW = 4


def narrow(a, b, dims):
    return product(halves(a), halves(b), dims)


def eliminate(part):
    groups, tiles = BS // 8, len(part[0])
    rows = lax.broadcasted_iota(jnp.int32, (8, 1), 0)
    scaled = [[None] * tiles for _ in range(groups)]

    def fetch(k, begin):
        return {g: jnp.broadcast_to(part[g][0][:, k : k + 1], (8, 128)) for g in range(begin, groups)}

    ahead = {k: fetch(k, 0) for k in range(2 * WINDOW)}
    for k in range(0, BS, 2):
        at, row = k // 8, k % 8
        first, second = ahead.pop(k), ahead.pop(k + 1)
        up = lambda x: pltpu.roll(x, 7, 0)
        a, b, d = first[at], second[at], up(second[at])
        inverse = 1.0 / (a * d - b * b)
        p, q, r = (x[row : row + 1, :] for x in (d * inverse, b * inverse, a * inverse))

        def solved(x):
            n = x.shape[1]
            low, x = up(x)[row : row + 1, :], x[row : row + 1, :]
            top, low = p[:, :n] * x - q[:, :n] * low, r[:, :n] * low - q[:, :n] * x
            return top, low

        if row < 6:
            keep = rows > row + 1
            first[at], second[at] = jnp.where(keep, first[at], 0.0), jnp.where(keep, second[at], 0.0)
            live = range(at, groups)
        else:
            live = range(at + 1, groups)
        for column in ahead.values():
            top, low = solved(column[at])
            for g in live:
                if g in column:
                    column[g] = column[g] - (first[g] * top + second[g] * low)
        for t in range(tiles):
            top, low = solved(part[at][t])
            n = top.shape[1]
            for g in live:
                part[g][t] = part[g][t] - (first[g][:, :n] * top + second[g][:, :n] * low)
            pair = jnp.where(rows == row, top, low)
            scaled[at][t] = pair if row == 0 else jnp.where(rows < row, scaled[at][t], pair)
        for late in (k + 2 * WINDOW, k + 2 * WINDOW + 1):
            if late < BS:
                ahead[late] = fetch(late, (k + 2) // 8)
    join = lambda x: [jnp.concatenate([x[g][t] for g in range(groups)], axis=0) for t in range(tiles)]
    return join(part), join(scaled)


def solve_kernel(sums_ref, stack_ref, update_hbm, residual_hbm, update_ref, residual_ref, update_sem, residual_sem):
    u = [sums_ref[64 * k : 64 * (k + 1), :] for k in range(7)]
    row = lax.broadcasted_iota(jnp.int32, (BS, 128), 0)
    lane = lax.broadcasted_iota(jnp.int32, (BS, 128), 1)
    eye = jnp.where(row == lane % BS, 1.0, 0.0)
    left = lane < BS
    half = lambda tiles, i: tiles[i // 2][:, 64 * (i % 2) : 64 * (i % 2 + 1)]
    tiles = {
        0: [u[0], u[1], jnp.where(left, u[6], eye)],
        1: [u[2], u[3], eye[:, 0:64]],
        2: [u[4], jnp.where(left, eye, u[6])],
        3: [u[5], eye[:, 0:64]],
    }
    order = {0: (0, 1, 2, 3, 4, 5), 1: (1, 2, 3, 4, 5), 2: (2, 3, 5, 4), 3: (3, 4, 5)}
    spans = [stack_ref[64 * k : 64 * (k + 1), :] for k in range(S)]
    both = None
    for k in range(S):
        part = [[t[8 * g : 8 * (g + 1), :] for t in tiles[k]] for g in range(BS // 8)]
        part, scaled = eliminate(part)
        y = {name: half(part, i) for i, name in enumerate(order[k])}
        z = {name: half(scaled, i) for i, name in enumerate(order[k])}
        for i in range(k + 1, S):
            names = [n for n in order[i] if n < 5]
            change = narrow(y[i], jnp.concatenate([z[n] for n in names], axis=1), ((0,), (0,)))
            fresh = []
            for t, tile in enumerate(tiles[i]):
                have = order[i][2 * t : 2 * t + 2]
                cut = [change[:, 64 * names.index(n) : 64 * (names.index(n) + 1)] if n < 5 else jnp.zeros((BS, BS), jnp.float32) for n in have]
                if all(n < 5 for n in have):
                    at = 64 * names.index(have[0])
                    fresh.append(tile - change[:, at : at + 64 * len(have)])
                elif any(n < 5 for n in have):
                    fresh.append(tile - jnp.concatenate(cut, axis=1))
                else:
                    fresh.append(tile)
            tiles[i] = fresh
        solved = narrow(y[5], jnp.concatenate([z[n] for n in range(k + 1, 5)], axis=1), ((0,), (0,)))
        term = [narrow(solved[:, 64 * (S - 1 - k) :], spans[k][:, 256 * h : 256 * (h + 1)], ((0,), (0,))) for h in (0, 1)]
        both = term if both is None else [b + t for b, t in zip(both, term)]
        for i in range(k + 1, S):
            spans[i] = spans[i] - narrow(solved[:, 64 * (i - k - 1) : 64 * (i - k)], spans[k], ((0,), (0,)))
    update_ref[...] = both[0]
    update = pltpu.make_async_copy(update_ref, update_hbm, update_sem)
    update.start()
    residual_ref[...] = stack_ref[0:64, 0:256] - both[1]
    residual = pltpu.make_async_copy(residual_ref, residual_hbm, residual_sem)
    residual.start()
    update.wait()
    residual.wait()


def call(kernel, outs, in_specs, scratch=(), name=None, space=VMEM):
    shapes = [jax.ShapeDtypeStruct(s, jnp.float32) for s in outs]
    specs = [space] * len(outs)
    return pl.pallas_call(
        kernel,
        out_shape=shapes if len(outs) > 1 else shapes[0],
        in_specs=in_specs,
        out_specs=specs if len(outs) > 1 else specs[0],
        scratch_shapes=list(scratch),
        name=name,
        compiler_params=pltpu.CompilerParams(vmem_limit_bytes=48 * 1024 * 1024),
    )


def pack(cols, right_side, blocks, total_blocks):
    kernel = functools.partial(pack_kernel, total_blocks)
    scratch = (
        pltpu.SMEM(cols.shape, jnp.int32),
        pltpu.VMEM(blocks.shape, jnp.float32),
        pltpu.SemaphoreType.DMA,
        pltpu.SemaphoreType.DMA((blocks.shape[0],)),
        pltpu.SemaphoreType.DMA,
    )
    arrays = [pltpu.with_memory_space_constraint(a, pltpu.HBM) for a in (cols, right_side, blocks)]
    return call(kernel, [(256, 256), (320, 128), (320, 128), (8, 128)], [HBM] * 3, scratch, name="pack")(*arrays)


def basis(flag, own, other, pair):
    return call(basis_kernel, [(512, 128), (256, 512)], [VMEM] * 4, name="basis")(flag, own, other, pair)


def total(parts, copies):
    kernel = functools.partial(total_kernel, copies)
    return call(kernel, [(copies,) + parts.shape[1:]], [VMEM], name="total")(parts)


def solve(sums, stack):
    scratch = [pltpu.VMEM((64, 256), jnp.float32)] * 2 + [pltpu.SemaphoreType.DMA] * 2
    return call(solve_kernel, [(64, 256), (64, 256)], [VMEM, VMEM], scratch, "solve", HBM)(sums, stack)


AXES = ("y", "z", "next", "x", "core")
NEAR = ("y", "next", "x", "core")


def shards(right_side, blocks, cols):
    devices = lax.axis_size(AXES)
    cols = cols.T
    own, other, pair, flag = pack(cols, right_side, blocks, cols.shape[0] * devices)
    other = lax.ppermute(other, AXES, [(i, ((i - 1) ^ 1) + 1) if 0 < i < devices - 1 else (i, devices - 1 - i) for i in range(devices)])
    pair = lax.ppermute(pair, AXES, [(i, i ^ 1) for i in range(devices)])
    sums, stack = basis(flag, own, other, pair)
    parts = lax.all_to_all(sums.reshape(64, 8, 128), NEAR, 0, 0)
    parts = lax.all_to_all(total(parts, 8), "z", 0, 0)
    sums = lax.all_to_all(total(parts, 64), NEAR, 0, 0)
    return tuple(solve(sums.reshape(512, 128), stack))


def solution(mesh):
    grid = Mesh(mesh.devices.reshape(4, 8, 2, 4, 2), AXES)
    in_specs = (P(None, AXES), P(None, None, AXES), P(None, AXES))
    out_specs = (P(None, AXES), P(None, AXES))
    return jax.shard_map(shards, mesh=grid, in_specs=in_specs, out_specs=out_specs, check_vma=False)
```

```python
import functools

import jax
import jax.numpy as jnp
from jax import lax
from jax.experimental import pallas as pl
from jax.experimental.pallas import tpu as pltpu
from jax.sharding import Mesh, PartitionSpec as P

SCALE = 1.25
S = 4
BS = 64

HBM = pl.BlockSpec(memory_space=pltpu.HBM)
VMEM = pl.BlockSpec(memory_space=pltpu.VMEM)
SMEM = pl.BlockSpec(memory_space=pltpu.SMEM)


def halves(a):
    high = a.astype(jnp.bfloat16)
    return high, (a - high.astype(jnp.float32)).astype(jnp.bfloat16)


def product(a, b, dims):
    one = lambda x, y: lax.dot_general(x, y, (dims, ((), ())), preferred_element_type=jnp.float32)
    return one(a[0], b[0]) + (one(a[0], b[1]) + one(a[1], b[0]))


def banded(minus, zero, plus):
    left = lax.broadcasted_iota(jnp.int32, (BS, 128), 1) < BS
    parts = [
        jnp.where(left, minus, 0.0),
        jnp.where(left, zero, minus),
        jnp.where(left, plus, zero),
        jnp.where(left, 0.0, plus),
    ]
    return halves(SCALE * jnp.concatenate(parts, axis=0))


def pack_kernel(total_blocks, cols_hbm, right_ref, blocks_ref, out_ref, other_ref, pair_ref, flag_ref, cols_ref, part_ref, cols_sem, part_sem, right_sem):
    slots, _, width = part_ref.shape
    table = pltpu.make_async_copy(cols_hbm, cols_ref, cols_sem)
    table.start()
    copies = [pltpu.make_async_copy(blocks_ref.at[slot], part_ref.at[slot], part_sem.at[slot]) for slot in range(slots)]
    for copy in copies:
        copy.start()
    last = pltpu.make_async_copy(right_ref, out_ref.at[192:256], right_sem)
    last.start()
    lane = lax.broadcasted_iota(jnp.int32, (1, width), 1) // BS
    table.wait()
    odd = lax.rem(cols_ref[0, 0] // (width // BS), 2)
    flag_ref[...] = jnp.full(flag_ref.shape, 1 - odd, jnp.int32).astype(jnp.float32)
    offsets = []
    for slot in (5, 6):
        offset = jnp.zeros((1, width), jnp.int32)
        for row in range(width // BS):
            delta = cols_ref[row, slot] - cols_ref[row, 0]
            delta = jnp.where(delta > 1, delta - total_blocks, delta)
            delta = jnp.where(delta < -1, delta + total_blocks, delta)
            offset = jnp.where(lane == row, delta, offset)
        offsets.append(offset)
    for copy in copies:
        copy.wait()
    inner = []
    for at, value, fixed in ((0, -1, (2, 4)), (64, 0, (0,)), (128, 1, (1, 3))):
        kept = sum(part_ref[slot] for slot in fixed)
        for slot, offset in zip((5, 6), offsets):
            kept = kept + jnp.where(offset == value, part_ref[slot], 0.0)
        out_ref[at : at + 64, :] = kept
        inner.append(pltpu.roll(kept, 64, 1)[:, 128:256])
    last.wait()
    image = product(halves(out_ref[192:256, :]), banded(*inner), ((1,), (0,)))
    even = jnp.full((1, 128), odd, jnp.int32) == 0
    head, tail = out_ref[:, 0:128], out_ref[:, 128:256]
    pair_ref[0:256, :] = jnp.where(even, tail, head)
    other_ref[0:256, :] = jnp.where(even, head, tail)
    pair_ref[256:320, :] = image
    other_ref[256:320, :] = image


def basis_kernel(flag_ref, own_ref, other_ref, pair_ref, sums_ref, stack_ref):
    even = flag_ref[0:1, :] > 0
    pair, other = pair_ref[...], other_ref[...]
    ends = jnp.where(even, other, pair), jnp.where(even, pair, other)
    parts = [ends[0], own_ref[:, 0:128], own_ref[:, 128:256], ends[1]]
    bands = [banded(part[0:64], part[64:128], part[128:192]) for part in parts]
    edges = [halves(end[256:320]) for end in ends]

    def rolled(tiles):
        both = halves(pltpu.roll(jnp.concatenate(tiles, axis=1), 64, 1))
        shifted = [tuple(r[:, 128 * p : 128 * (p + 1)] for r in both) for p in range(4)]
        return shifted + shifted[:1]

    tiles = [part[192:256] for part in parts]
    own = [jnp.concatenate(tiles[1:3], axis=1)]
    for step in range(S):
        shifted = rolled(tiles)
        if step == 1:
            shifted[0], shifted[4] = edges
        fresh = list(tiles)
        for p in range(4) if step < S - 1 else (1, 2):
            window = [jnp.concatenate([a, b], axis=1) for a, b in zip(shifted[p], shifted[p + 1])]
            fresh[p] = product(window, bands[p], ((1,), (0,)))
        tiles = fresh
        own.append(jnp.concatenate(tiles[1:3], axis=1))
    images = [own[k] + own[k + 1] / SCALE for k in range(S)]
    w = jnp.concatenate(images, axis=0)
    stack_ref[:, 0:256] = jnp.concatenate(own[:S], axis=0)
    stack_ref[:, 256:512] = w
    z = jnp.concatenate([w, own[0]], axis=0)
    z = halves(z)
    g = [product([h[64 * k : 64 * (k + 1)] for h in z], [h[64 * k :] for h in z], ((1,), (1,))) for k in range(S)]
    sums_ref[0:64, :] = g[0][:, 0:128]
    sums_ref[64:128, :] = g[0][:, 128:256]
    sums_ref[128:192, :] = g[1][:, 0:128]
    sums_ref[192:256, :] = g[1][:, 128:256]
    sums_ref[256:320, :] = g[2][:, 0:128]
    sums_ref[320:384, :] = g[3]
    sums_ref[384:448, :] = jnp.concatenate([g[0][:, 256:320], g[2][:, 128:192]], axis=1)
    sums_ref[448:512, :] = jnp.zeros((64, 128), jnp.float32)


def total_kernel(copies, in_ref, out_ref):
    total = in_ref[0]
    for k in range(1, in_ref.shape[0]):
        total = total + in_ref[k]
    for k in range(copies):
        out_ref[k] = total


WINDOW = 4


def narrow(a, b, dims):
    return product(halves(a), halves(b), dims)


def eliminate(part):
    groups, tiles = BS // 8, len(part[0])
    rows = lax.broadcasted_iota(jnp.int32, (8, 1), 0)
    scaled = [[None] * tiles for _ in range(groups)]

    def fetch(k, begin):
        return {g: jnp.broadcast_to(part[g][0][:, k : k + 1], (8, 128)) for g in range(begin, groups)}

    ahead = {k: fetch(k, 0) for k in range(2 * WINDOW)}
    for k in range(0, BS, 2):
        at, row = k // 8, k % 8
        first, second = ahead.pop(k), ahead.pop(k + 1)
        up = lambda x: pltpu.roll(x, 7, 0)
        a, b, d = first[at], up(first[at]), up(second[at])
        inverse = 1.0 / (a * d - b * b)
        p, q, r = (x[row : row + 1, :] for x in (d * inverse, b * inverse, a * inverse))

        def solved(x):
            n = x.shape[1]
            low, x = up(x)[row : row + 1, :], x[row : row + 1, :]
            top, low = p[:, :n] * x - q[:, :n] * low, r[:, :n] * low - q[:, :n] * x
            return top, low

        if row < 6:
            keep = rows > row + 1
            first[at], second[at] = jnp.where(keep, first[at], 0.0), jnp.where(keep, second[at], 0.0)
            live = range(at, groups)
        else:
            live = range(at + 1, groups)
        for column in ahead.values():
            top, low = solved(column[at])
            for g in live:
                if g in column:
                    column[g] = column[g] - (first[g] * top + second[g] * low)
        for t in range(tiles):
            top, low = solved(part[at][t])
            n = top.shape[1]
            for g in live:
                part[g][t] = part[g][t] - (first[g][:, :n] * top + second[g][:, :n] * low)
            pair = jnp.where(rows == row, top, low)
            scaled[at][t] = pair if row == 0 else jnp.where(rows < row, scaled[at][t], pair)
        for late in (k + 2 * WINDOW, k + 2 * WINDOW + 1):
            if late < BS:
                ahead[late] = fetch(late, (k + 2) // 8)
    join = lambda x: [jnp.concatenate([x[g][t] for g in range(groups)], axis=0) for t in range(tiles)]
    return join(part), join(scaled)


def solve_kernel(sums_ref, stack_ref, update_hbm, residual_hbm, update_ref, residual_ref, update_sem, residual_sem):
    place = lambda k, i: 128 * (k // 2) + 16 * i + 8 * (k % 2)
    u = [jnp.concatenate([sums_ref[place(k, i) : place(k, i) + 8, :] for i in range(8)], axis=0) for k in range(7)]
    row = lax.broadcasted_iota(jnp.int32, (BS, 128), 0)
    lane = lax.broadcasted_iota(jnp.int32, (BS, 128), 1)
    eye = jnp.where(row == lane % BS, 1.0, 0.0)
    left = lane < BS
    half = lambda tiles, i: tiles[i // 2][:, 64 * (i % 2) : 64 * (i % 2 + 1)]
    tiles = {
        0: [u[0], u[1], jnp.where(left, u[6], eye)],
        1: [u[2], u[3], eye[:, 0:64]],
        2: [u[4], jnp.where(left, eye, u[6])],
        3: [u[5], eye[:, 0:64]],
    }
    order = {0: (0, 1, 2, 3, 4, 5), 1: (1, 2, 3, 4, 5), 2: (2, 3, 5, 4), 3: (3, 4, 5)}
    spans = [stack_ref[64 * k : 64 * (k + 1), :] for k in range(S)]
    both = None
    for k in range(S):
        part = [[t[8 * g : 8 * (g + 1), :] for t in tiles[k]] for g in range(BS // 8)]
        part, scaled = eliminate(part)
        y = {name: half(part, i) for i, name in enumerate(order[k])}
        z = {name: half(scaled, i) for i, name in enumerate(order[k])}
        for i in range(k + 1, S):
            names = [n for n in order[i] if n < 5]
            change = narrow(y[i], jnp.concatenate([z[n] for n in names], axis=1), ((0,), (0,)))
            fresh = []
            for t, tile in enumerate(tiles[i]):
                have = order[i][2 * t : 2 * t + 2]
                cut = [change[:, 64 * names.index(n) : 64 * (names.index(n) + 1)] if n < 5 else jnp.zeros((BS, BS), jnp.float32) for n in have]
                if all(n < 5 for n in have):
                    at = 64 * names.index(have[0])
                    fresh.append(tile - change[:, at : at + 64 * len(have)])
                elif any(n < 5 for n in have):
                    fresh.append(tile - jnp.concatenate(cut, axis=1))
                else:
                    fresh.append(tile)
            tiles[i] = fresh
        solved = narrow(y[5], jnp.concatenate([z[n] for n in range(k + 1, 5)], axis=1), ((0,), (0,)))
        term = [narrow(solved[:, 64 * (S - 1 - k) :], spans[k][:, 256 * h : 256 * (h + 1)], ((0,), (0,))) for h in (0, 1)]
        both = term if both is None else [b + t for b, t in zip(both, term)]
        for i in range(k + 1, S):
            spans[i] = spans[i] - narrow(solved[:, 64 * (i - k - 1) : 64 * (i - k)], spans[k], ((0,), (0,)))
    update_ref[...] = both[0]
    update = pltpu.make_async_copy(update_ref, update_hbm, update_sem)
    update.start()
    residual_ref[...] = stack_ref[0:64, 0:256] - both[1]
    residual = pltpu.make_async_copy(residual_ref, residual_hbm, residual_sem)
    residual.start()
    update.wait()
    residual.wait()


def call(kernel, outs, in_specs, scratch=(), name=None, space=VMEM):
    shapes = [jax.ShapeDtypeStruct(s, jnp.float32) for s in outs]
    specs = [space] * len(outs)
    return pl.pallas_call(
        kernel,
        out_shape=shapes if len(outs) > 1 else shapes[0],
        in_specs=in_specs,
        out_specs=specs if len(outs) > 1 else specs[0],
        scratch_shapes=list(scratch),
        name=name,
        compiler_params=pltpu.CompilerParams(vmem_limit_bytes=48 * 1024 * 1024),
    )


def pack(cols, right_side, blocks, total_blocks):
    kernel = functools.partial(pack_kernel, total_blocks)
    scratch = (
        pltpu.SMEM(cols.shape, jnp.int32),
        pltpu.VMEM(blocks.shape, jnp.float32),
        pltpu.SemaphoreType.DMA,
        pltpu.SemaphoreType.DMA((blocks.shape[0],)),
        pltpu.SemaphoreType.DMA,
    )
    arrays = [pltpu.with_memory_space_constraint(a, pltpu.HBM) for a in (cols, right_side, blocks)]
    return call(kernel, [(256, 256), (320, 128), (320, 128), (8, 128)], [HBM] * 3, scratch, name="pack")(*arrays)


def basis(flag, own, other, pair):
    return call(basis_kernel, [(512, 128), (256, 512)], [VMEM] * 4, name="basis")(flag, own, other, pair)


def total(parts, copies):
    kernel = functools.partial(total_kernel, copies)
    return call(kernel, [(copies,) + parts.shape[1:]], [VMEM], name="total")(parts)


def solve(sums, stack):
    scratch = [pltpu.VMEM((64, 256), jnp.float32)] * 2 + [pltpu.SemaphoreType.DMA] * 2
    return call(solve_kernel, [(64, 256), (64, 256)], [VMEM, VMEM], scratch, "solve", HBM)(sums, stack)


AXES = ("y", "z", "next", "x", "core")


def shards(right_side, blocks, cols):
    devices = lax.axis_size(AXES)
    cols = cols.T
    own, other, pair, flag = pack(cols, right_side, blocks, cols.shape[0] * devices)
    other = lax.ppermute(other, AXES, [(i, ((i - 1) ^ 1) + 1) if 0 < i < devices - 1 else (i, devices - 1 - i) for i in range(devices)])
    pair = lax.ppermute(pair, AXES, [(i, i ^ 1) for i in range(devices)])
    sums, stack = basis(flag, own, other, pair)
    parts = lax.all_to_all(sums.reshape(64, 8, 128), ("y", "next", "x", "core"), 0, 0)
    parts = lax.all_to_all(total(parts, 16), ("z", "next"), 0, 0)
    sums = lax.all_to_all(total(parts.reshape(8, 16, 128), 32), ("y", "x", "core"), 0, 0)
    return tuple(solve(sums.reshape(512, 128), stack))


def solution(mesh):
    grid = Mesh(mesh.devices.reshape(4, 8, 2, 4, 2), AXES)
    in_specs = (P(None, AXES), P(None, None, AXES), P(None, AXES))
    out_specs = (P(None, AXES), P(None, AXES))
    return jax.shard_map(shards, mesh=grid, in_specs=in_specs, out_specs=out_specs, check_vma=False)
```

```python
import functools

import jax
import jax.numpy as jnp
from jax import lax
from jax.experimental import pallas as pl
from jax.experimental.pallas import tpu as pltpu
from jax.sharding import Mesh, PartitionSpec as P

SCALE = 1.25
S = 4
BS = 64

HBM = pl.BlockSpec(memory_space=pltpu.HBM)
VMEM = pl.BlockSpec(memory_space=pltpu.VMEM)
SMEM = pl.BlockSpec(memory_space=pltpu.SMEM)


def halves(a):
    high = a.astype(jnp.bfloat16)
    return high, (a - high.astype(jnp.float32)).astype(jnp.bfloat16)


def product(a, b, dims):
    one = lambda x, y: lax.dot_general(x, y, (dims, ((), ())), preferred_element_type=jnp.float32)
    return one(a[0], b[0]) + (one(a[0], b[1]) + one(a[1], b[0]))


def banded(minus, zero, plus):
    left = lax.broadcasted_iota(jnp.int32, (BS, 128), 1) < BS
    parts = [
        jnp.where(left, minus, 0.0),
        jnp.where(left, zero, minus),
        jnp.where(left, plus, zero),
        jnp.where(left, 0.0, plus),
    ]
    return halves(SCALE * jnp.concatenate(parts, axis=0))


def pack_kernel(total_blocks, cols_hbm, right_ref, blocks_ref, out_ref, other_ref, pair_ref, flag_ref, cols_ref, part_ref, cols_sem, part_sem, right_sem):
    slots, _, width = part_ref.shape
    table = pltpu.make_async_copy(cols_hbm, cols_ref, cols_sem)
    table.start()
    copies = [pltpu.make_async_copy(blocks_ref.at[slot], part_ref.at[slot], part_sem.at[slot]) for slot in range(slots)]
    for copy in copies:
        copy.start()
    last = pltpu.make_async_copy(right_ref, out_ref.at[192:256], right_sem)
    last.start()
    lane = lax.broadcasted_iota(jnp.int32, (1, width), 1) // BS
    table.wait()
    odd = lax.rem(cols_ref[0, 0] // (width // BS), 2)
    flag_ref[...] = jnp.full(flag_ref.shape, 1 - odd, jnp.int32).astype(jnp.float32)
    offsets = []
    for slot in (5, 6):
        offset = jnp.zeros((1, width), jnp.int32)
        for row in range(width // BS):
            delta = cols_ref[row, slot] - cols_ref[row, 0]
            delta = jnp.where(delta > 1, delta - total_blocks, delta)
            delta = jnp.where(delta < -1, delta + total_blocks, delta)
            offset = jnp.where(lane == row, delta, offset)
        offsets.append(offset)
    for copy in copies:
        copy.wait()
    inner = []
    for at, value, fixed in ((0, -1, (2, 4)), (64, 0, (0,)), (128, 1, (1, 3))):
        kept = sum(part_ref[slot] for slot in fixed)
        for slot, offset in zip((5, 6), offsets):
            kept = kept + jnp.where(offset == value, part_ref[slot], 0.0)
        out_ref[at : at + 64, :] = kept
        inner.append(pltpu.roll(kept, 64, 1)[:, 128:256])
    last.wait()
    image = product(halves(out_ref[192:256, :]), banded(*inner), ((1,), (0,)))
    even = jnp.full((1, 128), odd, jnp.int32) == 0
    head, tail = out_ref[:, 0:128], out_ref[:, 128:256]
    pair_ref[0:256, :] = jnp.where(even, tail, head)
    other_ref[0:256, :] = jnp.where(even, head, tail)
    pair_ref[256:320, :] = image
    other_ref[256:320, :] = image


def basis_kernel(flag_ref, own_ref, other_ref, pair_ref, sums_ref, stack_ref):
    even = flag_ref[0:1, :] > 0
    pair, other = pair_ref[...], other_ref[...]
    ends = jnp.where(even, other, pair), jnp.where(even, pair, other)
    parts = [ends[0], own_ref[:, 0:128], own_ref[:, 128:256], ends[1]]
    bands = [banded(part[0:64], part[64:128], part[128:192]) for part in parts]
    edges = [halves(end[256:320]) for end in ends]

    def rolled(tiles):
        both = halves(pltpu.roll(jnp.concatenate(tiles, axis=1), 64, 1))
        shifted = [tuple(r[:, 128 * p : 128 * (p + 1)] for r in both) for p in range(4)]
        return shifted + shifted[:1]

    tiles = [part[192:256] for part in parts]
    own = [jnp.concatenate(tiles[1:3], axis=1)]
    for step in range(S):
        shifted = rolled(tiles)
        if step == 1:
            shifted[0], shifted[4] = edges
        fresh = list(tiles)
        for p in range(4) if step < S - 1 else (1, 2):
            window = [jnp.concatenate([a, b], axis=1) for a, b in zip(shifted[p], shifted[p + 1])]
            fresh[p] = product(window, bands[p], ((1,), (0,)))
        tiles = fresh
        own.append(jnp.concatenate(tiles[1:3], axis=1))
    images = [own[k] + own[k + 1] / SCALE for k in range(S)]
    w = jnp.concatenate(images, axis=0)
    stack_ref[:, 0:256] = jnp.concatenate(own[:S], axis=0)
    stack_ref[:, 256:512] = w
    z = jnp.concatenate([w, own[0]], axis=0)
    z = halves(z)
    g = [product([h[64 * k : 64 * (k + 1)] for h in z], [h[64 * k :] for h in z], ((1,), (1,))) for k in range(S)]
    sums_ref[0:64, :] = g[0][:, 0:128]
    sums_ref[64:128, :] = g[0][:, 128:256]
    sums_ref[128:192, :] = g[1][:, 0:128]
    sums_ref[192:256, :] = g[1][:, 128:256]
    sums_ref[256:320, :] = g[2][:, 0:128]
    sums_ref[320:384, :] = g[3]
    sums_ref[384:448, :] = jnp.concatenate([g[0][:, 256:320], g[2][:, 128:192]], axis=1)
    sums_ref[448:512, :] = jnp.zeros((64, 128), jnp.float32)


def total_kernel(copies, in_ref, out_ref):
    total = in_ref[0]
    for k in range(1, in_ref.shape[0]):
        total = total + in_ref[k]
    for k in range(copies):
        out_ref[k] = total


WINDOW = 4


def narrow(a, b, dims):
    return product(halves(a), halves(b), dims)


def eliminate(part):
    groups, tiles = BS // 8, len(part[0])
    rows = lax.broadcasted_iota(jnp.int32, (8, 1), 0)
    scaled = [[None] * tiles for _ in range(groups)]

    def fetch(k, begin):
        return {g: jnp.broadcast_to(part[g][0][:, k : k + 1], (8, 128)) for g in range(begin, groups)}

    ahead = {k: fetch(k, 0) for k in range(2 * WINDOW)}
    for k in range(0, BS, 2):
        at, row = k // 8, k % 8
        first, second = ahead.pop(k), ahead.pop(k + 1)
        up = lambda x: pltpu.roll(x, 7, 0)
        a, b, d = first[at], up(first[at]), up(second[at])
        inverse = 1.0 / (a * d - b * b)
        p, q, r = (x[row : row + 1, :] for x in (d * inverse, b * inverse, a * inverse))

        def solved(x):
            n = x.shape[1]
            low, x = up(x)[row : row + 1, :], x[row : row + 1, :]
            top, low = p[:, :n] * x - q[:, :n] * low, r[:, :n] * low - q[:, :n] * x
            return top, low

        if row < 6:
            keep = rows > row + 1
            first[at], second[at] = jnp.where(keep, first[at], 0.0), jnp.where(keep, second[at], 0.0)
            live = range(at, groups)
        else:
            live = range(at + 1, groups)
        for column in ahead.values():
            top, low = solved(column[at])
            for g in live:
                if g in column:
                    column[g] = column[g] - (first[g] * top + second[g] * low)
        for t in range(tiles):
            top, low = solved(part[at][t])
            n = top.shape[1]
            for g in live:
                part[g][t] = part[g][t] - (first[g][:, :n] * top + second[g][:, :n] * low)
            pair = jnp.where(rows == row, top, low)
            scaled[at][t] = pair if row == 0 else jnp.where(rows < row, scaled[at][t], pair)
        for late in (k + 2 * WINDOW, k + 2 * WINDOW + 1):
            if late < BS:
                ahead[late] = fetch(late, (k + 2) // 8)
    join = lambda x: [jnp.concatenate([x[g][t] for g in range(groups)], axis=0) for t in range(tiles)]
    return join(part), join(scaled)


def solve_kernel(sums_ref, stack_ref, update_hbm, residual_hbm, update_ref, residual_ref, update_sem, residual_sem):
    u = [sums_ref[64 * k : 64 * (k + 1), :] for k in range(7)]
    row = lax.broadcasted_iota(jnp.int32, (BS, 128), 0)
    lane = lax.broadcasted_iota(jnp.int32, (BS, 128), 1)
    eye = jnp.where(row == lane % BS, 1.0, 0.0)
    left = lane < BS
    half = lambda tiles, i: tiles[i // 2][:, 64 * (i % 2) : 64 * (i % 2 + 1)]
    tiles = {
        0: [u[0], u[1], jnp.where(left, u[6], eye)],
        1: [u[2], u[3], eye[:, 0:64]],
        2: [u[4], jnp.where(left, eye, u[6])],
        3: [u[5], eye[:, 0:64]],
    }
    order = {0: (0, 1, 2, 3, 4, 5), 1: (1, 2, 3, 4, 5), 2: (2, 3, 5, 4), 3: (3, 4, 5)}
    spans = [stack_ref[64 * k : 64 * (k + 1), :] for k in range(S)]
    both = None
    for k in range(S):
        part = [[t[8 * g : 8 * (g + 1), :] for t in tiles[k]] for g in range(BS // 8)]
        part, scaled = eliminate(part)
        y = {name: half(part, i) for i, name in enumerate(order[k])}
        z = {name: half(scaled, i) for i, name in enumerate(order[k])}
        for i in range(k + 1, S):
            names = [n for n in order[i] if n < 5]
            change = narrow(y[i], jnp.concatenate([z[n] for n in names], axis=1), ((0,), (0,)))
            fresh = []
            for t, tile in enumerate(tiles[i]):
                have = order[i][2 * t : 2 * t + 2]
                cut = [change[:, 64 * names.index(n) : 64 * (names.index(n) + 1)] if n < 5 else jnp.zeros((BS, BS), jnp.float32) for n in have]
                if all(n < 5 for n in have):
                    at = 64 * names.index(have[0])
                    fresh.append(tile - change[:, at : at + 64 * len(have)])
                elif any(n < 5 for n in have):
                    fresh.append(tile - jnp.concatenate(cut, axis=1))
                else:
                    fresh.append(tile)
            tiles[i] = fresh
        solved = narrow(y[5], jnp.concatenate([z[n] for n in range(k + 1, 5)], axis=1), ((0,), (0,)))
        term = [narrow(solved[:, 64 * (S - 1 - k) :], spans[k][:, 256 * h : 256 * (h + 1)], ((0,), (0,))) for h in (0, 1)]
        both = term if both is None else [b + t for b, t in zip(both, term)]
        for i in range(k + 1, S):
            spans[i] = spans[i] - narrow(solved[:, 64 * (i - k - 1) : 64 * (i - k)], spans[k], ((0,), (0,)))
    update_ref[...] = both[0]
    update = pltpu.make_async_copy(update_ref, update_hbm, update_sem)
    update.start()
    residual_ref[...] = stack_ref[0:64, 0:256] - both[1]
    residual = pltpu.make_async_copy(residual_ref, residual_hbm, residual_sem)
    residual.start()
    update.wait()
    residual.wait()


def call(kernel, outs, in_specs, scratch=(), name=None, space=VMEM):
    shapes = [jax.ShapeDtypeStruct(s, jnp.float32) for s in outs]
    specs = [space] * len(outs)
    return pl.pallas_call(
        kernel,
        out_shape=shapes if len(outs) > 1 else shapes[0],
        in_specs=in_specs,
        out_specs=specs if len(outs) > 1 else specs[0],
        scratch_shapes=list(scratch),
        name=name,
        compiler_params=pltpu.CompilerParams(vmem_limit_bytes=48 * 1024 * 1024),
    )


def pack(cols, right_side, blocks, total_blocks):
    kernel = functools.partial(pack_kernel, total_blocks)
    scratch = (
        pltpu.SMEM(cols.shape, jnp.int32),
        pltpu.VMEM(blocks.shape, jnp.float32),
        pltpu.SemaphoreType.DMA,
        pltpu.SemaphoreType.DMA((blocks.shape[0],)),
        pltpu.SemaphoreType.DMA,
    )
    arrays = [pltpu.with_memory_space_constraint(a, pltpu.HBM) for a in (cols, right_side, blocks)]
    return call(kernel, [(256, 256), (320, 128), (320, 128), (8, 128)], [HBM] * 3, scratch, name="pack")(*arrays)


def basis(flag, own, other, pair):
    return call(basis_kernel, [(512, 128), (256, 512)], [VMEM] * 4, name="basis")(flag, own, other, pair)


def total(parts, copies):
    kernel = functools.partial(total_kernel, copies)
    return call(kernel, [(copies,) + parts.shape[1:]], [VMEM], name="total")(parts)


def solve(sums, stack):
    scratch = [pltpu.VMEM((64, 256), jnp.float32)] * 2 + [pltpu.SemaphoreType.DMA] * 2
    return call(solve_kernel, [(64, 256), (64, 256)], [VMEM, VMEM], scratch, "solve", HBM)(sums, stack)


AXES = ("y", "z", "x", "core")
PLANE = ("y", "x", "core")


def shards(right_side, blocks, cols):
    devices = lax.axis_size(AXES)
    cols = cols.T
    own, other, pair, flag = pack(cols, right_side, blocks, cols.shape[0] * devices)
    other = lax.ppermute(other, AXES, [(i, ((i - 1) ^ 1) + 1) if 0 < i < devices - 1 else (i, devices - 1 - i) for i in range(devices)])
    pair = lax.ppermute(pair, AXES, [(i, i ^ 1) for i in range(devices)])
    sums, stack = basis(flag, own, other, pair)
    parts = lax.all_to_all(sums.reshape(32, 16, 128), PLANE, 0, 0)
    parts = lax.all_to_all(total(parts, 16), "z", 0, 0)
    sums = lax.all_to_all(total(parts, 32), PLANE, 0, 0)
    return tuple(solve(sums.reshape(512, 128), stack))


def solution(mesh):
    grid = Mesh(mesh.devices.reshape(4, 16, 4, 2), AXES)
    in_specs = (P(None, AXES), P(None, None, AXES), P(None, AXES))
    out_specs = (P(None, AXES), P(None, AXES))
    return jax.shard_map(shards, mesh=grid, in_specs=in_specs, out_specs=out_specs, check_vma=False)
```

```python
import functools

import jax
import jax.numpy as jnp
from jax import lax
from jax.experimental import pallas as pl
from jax.experimental.pallas import tpu as pltpu
from jax.sharding import Mesh, PartitionSpec as P

SCALE = 1.25
S = 4
BS = 64

HBM = pl.BlockSpec(memory_space=pltpu.HBM)
VMEM = pl.BlockSpec(memory_space=pltpu.VMEM)
SMEM = pl.BlockSpec(memory_space=pltpu.SMEM)


def halves(a):
    high = a.astype(jnp.bfloat16)
    return high, (a - high.astype(jnp.float32)).astype(jnp.bfloat16)


def product(a, b, dims):
    one = lambda x, y: lax.dot_general(x, y, (dims, ((), ())), preferred_element_type=jnp.float32)
    return one(a[0], b[0]) + (one(a[0], b[1]) + one(a[1], b[0]))


def banded(minus, zero, plus):
    left = lax.broadcasted_iota(jnp.int32, (BS, 128), 1) < BS
    parts = [
        jnp.where(left, minus, 0.0),
        jnp.where(left, zero, minus),
        jnp.where(left, plus, zero),
        jnp.where(left, 0.0, plus),
    ]
    return halves(SCALE * jnp.concatenate(parts, axis=0))


def pack_kernel(total_blocks, cols_hbm, right_ref, blocks_ref, out_ref, other_ref, pair_ref, flag_ref, cols_ref, part_ref, cols_sem, part_sem, right_sem):
    slots, _, width = part_ref.shape
    table = pltpu.make_async_copy(cols_hbm, cols_ref, cols_sem)
    table.start()
    copies = [pltpu.make_async_copy(blocks_ref.at[slot], part_ref.at[slot], part_sem.at[slot]) for slot in range(slots)]
    for copy in copies:
        copy.start()
    last = pltpu.make_async_copy(right_ref, out_ref.at[192:256], right_sem)
    last.start()
    lane = lax.broadcasted_iota(jnp.int32, (1, width), 1) // BS
    table.wait()
    odd = lax.rem(cols_ref[0, 0] // (width // BS), 2)
    flag_ref[...] = jnp.full(flag_ref.shape, 1 - odd, jnp.int32).astype(jnp.float32)
    offsets = []
    for slot in (5, 6):
        offset = jnp.zeros((1, width), jnp.int32)
        for row in range(width // BS):
            delta = cols_ref[row, slot] - cols_ref[row, 0]
            delta = jnp.where(delta > 1, delta - total_blocks, delta)
            delta = jnp.where(delta < -1, delta + total_blocks, delta)
            offset = jnp.where(lane == row, delta, offset)
        offsets.append(offset)
    for copy in copies:
        copy.wait()
    inner = []
    for at, value, fixed in ((0, -1, (2, 4)), (64, 0, (0,)), (128, 1, (1, 3))):
        kept = sum(part_ref[slot] for slot in fixed)
        for slot, offset in zip((5, 6), offsets):
            kept = kept + jnp.where(offset == value, part_ref[slot], 0.0)
        out_ref[at : at + 64, :] = kept
        inner.append(pltpu.roll(kept, 64, 1)[:, 128:256])
    last.wait()
    image = product(halves(out_ref[192:256, :]), banded(*inner), ((1,), (0,)))
    even = jnp.full((1, 128), odd, jnp.int32) == 0
    head, tail = out_ref[:, 0:128], out_ref[:, 128:256]
    pair_ref[0:256, :] = jnp.where(even, tail, head)
    other_ref[0:256, :] = jnp.where(even, head, tail)
    pair_ref[256:320, :] = image
    other_ref[256:320, :] = image


def basis_kernel(flag_ref, own_ref, other_ref, pair_ref, sums_ref, stack_ref):
    even = flag_ref[0:1, :] > 0
    pair, other = pair_ref[...], other_ref[...]
    ends = jnp.where(even, other, pair), jnp.where(even, pair, other)
    parts = [ends[0], own_ref[:, 0:128], own_ref[:, 128:256], ends[1]]
    bands = [banded(part[0:64], part[64:128], part[128:192]) for part in parts]
    edges = [halves(end[256:320]) for end in ends]

    def rolled(tiles):
        both = halves(pltpu.roll(jnp.concatenate(tiles, axis=1), 64, 1))
        shifted = [tuple(r[:, 128 * p : 128 * (p + 1)] for r in both) for p in range(4)]
        return shifted + shifted[:1]

    tiles = [part[192:256] for part in parts]
    own = [jnp.concatenate(tiles[1:3], axis=1)]
    for step in range(S):
        shifted = rolled(tiles)
        if step == 1:
            shifted[0], shifted[4] = edges
        fresh = list(tiles)
        for p in range(4) if step < S - 1 else (1, 2):
            window = [jnp.concatenate([a, b], axis=1) for a, b in zip(shifted[p], shifted[p + 1])]
            fresh[p] = product(window, bands[p], ((1,), (0,)))
        tiles = fresh
        own.append(jnp.concatenate(tiles[1:3], axis=1))
    images = [own[k] + own[k + 1] / SCALE for k in range(S)]
    w = jnp.concatenate(images, axis=0)
    stack_ref[:, 0:256] = jnp.concatenate(own[:S], axis=0)
    stack_ref[:, 256:512] = w
    z = jnp.concatenate([w, own[0]], axis=0)
    z = halves(z)
    g = [product([h[64 * k : 64 * (k + 1)] for h in z], [h[64 * k :] for h in z], ((1,), (1,))) for k in range(S)]
    sums_ref[0:64, :] = g[0][:, 0:128]
    sums_ref[64:128, :] = g[0][:, 128:256]
    sums_ref[128:192, :] = g[1][:, 0:128]
    sums_ref[192:256, :] = g[1][:, 128:256]
    sums_ref[256:320, :] = g[2][:, 0:128]
    sums_ref[320:384, :] = g[3]
    sums_ref[384:448, :] = jnp.concatenate([g[0][:, 256:320], g[2][:, 128:192]], axis=1)
    sums_ref[448:512, :] = jnp.zeros((64, 128), jnp.float32)


def total_kernel(copies, in_ref, out_ref):
    total = in_ref[0]
    for k in range(1, in_ref.shape[0]):
        total = total + in_ref[k]
    for k in range(copies):
        out_ref[k] = total


WINDOW = 4


def narrow(a, b, dims):
    return product(halves(a), halves(b), dims)


def eliminate(part):
    groups, tiles = BS // 8, len(part[0])
    rows = lax.broadcasted_iota(jnp.int32, (8, 1), 0)
    scaled = [[None] * tiles for _ in range(groups)]

    def fetch(k, begin):
        return {g: jnp.broadcast_to(part[g][0][:, k : k + 1], (8, 128)) for g in range(begin, groups)}

    ahead = {k: fetch(k, 0) for k in range(2 * WINDOW)}
    for k in range(0, BS, 2):
        at, row = k // 8, k % 8
        first, second = ahead.pop(k), ahead.pop(k + 1)
        up = lambda x: pltpu.roll(x, 7, 0)
        a, b, d = first[at], up(first[at]), up(second[at])
        inverse = 1.0 / (a * d - b * b)
        p, q, r = (x[row : row + 1, :] for x in (d * inverse, b * inverse, a * inverse))

        def solved(x):
            n = x.shape[1]
            low, x = up(x)[row : row + 1, :], x[row : row + 1, :]
            top, low = p[:, :n] * x - q[:, :n] * low, r[:, :n] * low - q[:, :n] * x
            return top, low

        if row < 6:
            keep = rows > row + 1
            first[at], second[at] = jnp.where(keep, first[at], 0.0), jnp.where(keep, second[at], 0.0)
            live = range(at, groups)
        else:
            live = range(at + 1, groups)
        for column in ahead.values():
            top, low = solved(column[at])
            for g in live:
                if g in column:
                    column[g] = column[g] - first[g] * top - second[g] * low
        for t in range(tiles):
            top, low = solved(part[at][t])
            n = top.shape[1]
            for g in live:
                part[g][t] = part[g][t] - first[g][:, :n] * top - second[g][:, :n] * low
            pair = jnp.where(rows == row, top, low)
            scaled[at][t] = pair if row == 0 else jnp.where(rows < row, scaled[at][t], pair)
        for late in (k + 2 * WINDOW, k + 2 * WINDOW + 1):
            if late < BS:
                ahead[late] = fetch(late, (k + 2) // 8)
    join = lambda x: [jnp.concatenate([x[g][t] for g in range(groups)], axis=0) for t in range(tiles)]
    return join(part), join(scaled)


def solve_kernel(sums_ref, stack_ref, update_hbm, residual_hbm, update_ref, residual_ref, update_sem, residual_sem):
    u = [sums_ref[64 * k : 64 * (k + 1), :] for k in range(7)]
    row = lax.broadcasted_iota(jnp.int32, (BS, 128), 0)
    lane = lax.broadcasted_iota(jnp.int32, (BS, 128), 1)
    eye = jnp.where(row == lane % BS, 1.0, 0.0)
    left = lane < BS
    half = lambda tiles, i: tiles[i // 2][:, 64 * (i % 2) : 64 * (i % 2 + 1)]
    tiles = {
        0: [u[0], u[1], jnp.where(left, u[6], eye)],
        1: [u[2], u[3], eye[:, 0:64]],
        2: [u[4], jnp.where(left, eye, u[6])],
        3: [u[5], eye[:, 0:64]],
    }
    order = {0: (0, 1, 2, 3, 4, 5), 1: (1, 2, 3, 4, 5), 2: (2, 3, 5, 4), 3: (3, 4, 5)}
    spans = [stack_ref[64 * k : 64 * (k + 1), :] for k in range(S)]
    both = None
    for k in range(S):
        part = [[t[8 * g : 8 * (g + 1), :] for t in tiles[k]] for g in range(BS // 8)]
        part, scaled = eliminate(part)
        y = {name: half(part, i) for i, name in enumerate(order[k])}
        z = {name: half(scaled, i) for i, name in enumerate(order[k])}
        for i in range(k + 1, S):
            names = [n for n in order[i] if n < 5]
            change = narrow(y[i], jnp.concatenate([z[n] for n in names], axis=1), ((0,), (0,)))
            fresh = []
            for t, tile in enumerate(tiles[i]):
                have = order[i][2 * t : 2 * t + 2]
                cut = [change[:, 64 * names.index(n) : 64 * (names.index(n) + 1)] if n < 5 else jnp.zeros((BS, BS), jnp.float32) for n in have]
                if all(n < 5 for n in have):
                    at = 64 * names.index(have[0])
                    fresh.append(tile - change[:, at : at + 64 * len(have)])
                elif any(n < 5 for n in have):
                    fresh.append(tile - jnp.concatenate(cut, axis=1))
                else:
                    fresh.append(tile)
            tiles[i] = fresh
        solved = narrow(y[5], jnp.concatenate([z[n] for n in range(k + 1, 5)], axis=1), ((0,), (0,)))
        term = [narrow(solved[:, 64 * (S - 1 - k) :], spans[k][:, 256 * h : 256 * (h + 1)], ((0,), (0,))) for h in (0, 1)]
        both = term if both is None else [b + t for b, t in zip(both, term)]
        for i in range(k + 1, S):
            spans[i] = spans[i] - narrow(solved[:, 64 * (i - k - 1) : 64 * (i - k)], spans[k], ((0,), (0,)))
    update_ref[...] = both[0]
    update = pltpu.make_async_copy(update_ref, update_hbm, update_sem)
    update.start()
    residual_ref[...] = stack_ref[0:64, 0:256] - both[1]
    residual = pltpu.make_async_copy(residual_ref, residual_hbm, residual_sem)
    residual.start()
    update.wait()
    residual.wait()


def call(kernel, outs, in_specs, scratch=(), name=None, space=VMEM):
    shapes = [jax.ShapeDtypeStruct(s, jnp.float32) for s in outs]
    specs = [space] * len(outs)
    return pl.pallas_call(
        kernel,
        out_shape=shapes if len(outs) > 1 else shapes[0],
        in_specs=in_specs,
        out_specs=specs if len(outs) > 1 else specs[0],
        scratch_shapes=list(scratch),
        name=name,
        compiler_params=pltpu.CompilerParams(vmem_limit_bytes=48 * 1024 * 1024),
    )


def pack(cols, right_side, blocks, total_blocks):
    kernel = functools.partial(pack_kernel, total_blocks)
    scratch = (
        pltpu.SMEM(cols.shape, jnp.int32),
        pltpu.VMEM(blocks.shape, jnp.float32),
        pltpu.SemaphoreType.DMA,
        pltpu.SemaphoreType.DMA((blocks.shape[0],)),
        pltpu.SemaphoreType.DMA,
    )
    arrays = [pltpu.with_memory_space_constraint(a, pltpu.HBM) for a in (cols, right_side, blocks)]
    return call(kernel, [(256, 256), (320, 128), (320, 128), (8, 128)], [HBM] * 3, scratch, name="pack")(*arrays)


def basis(flag, own, other, pair):
    return call(basis_kernel, [(512, 128), (256, 512)], [VMEM] * 4, name="basis")(flag, own, other, pair)


def total(parts, copies):
    kernel = functools.partial(total_kernel, copies)
    return call(kernel, [(copies,) + parts.shape[1:]], [VMEM], name="total")(parts)


def solve(sums, stack):
    scratch = [pltpu.VMEM((64, 256), jnp.float32)] * 2 + [pltpu.SemaphoreType.DMA] * 2
    return call(solve_kernel, [(64, 256), (64, 256)], [VMEM, VMEM], scratch, "solve", HBM)(sums, stack)


AXES = ("y", "z", "x", "core")
PLANE = ("y", "x", "core")


def shards(right_side, blocks, cols):
    devices = lax.axis_size(AXES)
    cols = cols.T
    own, other, pair, flag = pack(cols, right_side, blocks, cols.shape[0] * devices)
    other = lax.ppermute(other, AXES, [(i, ((i - 1) ^ 1) + 1) if 0 < i < devices - 1 else (i, devices - 1 - i) for i in range(devices)])
    pair = lax.ppermute(pair, AXES, [(i, i ^ 1) for i in range(devices)])
    sums, stack = basis(flag, own, other, pair)
    parts = lax.all_to_all(sums.reshape(32, 16, 128), PLANE, 0, 0)
    parts = lax.all_to_all(total(parts, 16), "z", 0, 0)
    sums = lax.all_to_all(total(parts, 32), PLANE, 0, 0)
    return tuple(solve(sums.reshape(512, 128), stack))


def solution(mesh):
    grid = Mesh(mesh.devices.reshape(4, 16, 4, 2), AXES)
    in_specs = (P(None, AXES), P(None, None, AXES), P(None, AXES))
    out_specs = (P(None, AXES), P(None, AXES))
    return jax.shard_map(shards, mesh=grid, in_specs=in_specs, out_specs=out_specs, check_vma=False)
```
